32 devices in a mesh: gx: 8 (over y, x, core), gy: 4 (over z).
Axes of the slice: x: 2, y: 2, z: 4, core: 2. Of those that a mesh axis runs over, the one named last changes fastest.
Arguments:
- states: bfloat16 [512, 2048], P('gx'), may hold values from -6 to 6
- attn_gain: bfloat16 [2048], replicated, may hold values from 0.099609375 to 1.8984375
- w_qkv: bfloat16 [2048, 5120], P(None, 'gy'), may hold values from -0.125 to 0.125
- q_gain: bfloat16 [128], replicated, may hold values from 0.099609375 to 1.8984375
- k_gain: bfloat16 [128], replicated, may hold values from 0.099609375 to 1.8984375
- cache_k: bfloat16 [8, 4096, 512], P('gx', 'gy'), may hold values from -400 to 400
- cache_v: bfloat16 [8, 4096, 512], P('gx', 'gy'), may hold values from -6 to 6
- cache_len: int32 [8], P('gx'), may hold values from 256 to 4096, as said below
- tree_mask: int32 [8, 64, 64], P('gx'), may hold values from 0 to 1, as said below
- w_o: bfloat16 [4096, 2048], P(None, 'gy'), may hold values from -0.09375 to 0.09375
- ffn_gain: bfloat16 [2048], P('gy'), may hold values from 0.099609375 to 1.8984375
- routing: int32 [512, 8], replicated, may hold values from 0 to 63, all different within a row; in each aligned block of 64 rows (0 to 63, 64 to 127, ...) at most 12 rows name the same one
- route_weight: float32 [512, 8], replicated, may hold values from 0.05 to 0.5
- w_in: bfloat16 [64, 2048, 1536], P('gx', 'gy'), may hold values from -0.125 to 0.125
- w_down: bfloat16 [64, 768, 2048], P('gx', None, 'gy'), may hold values from -0.21875 to 0.21875
- accept: int32 [8, 8, 64], P('gx'), may hold values from 0 to 1, as said below
Outputs:
- layer_out: bfloat16 [512, 2048], P('gx', 'gy')
- accepted_kv: bfloat16 [8, 8, 1024], P('gx')
The draws below stay inside these ranges and needn't reach their ends.
Inputs may be any that keep to these rules, and one draw needn't show every extreme that they name: `cache_len`: each request's cache holds keys at positions below its length; some request fills all 4096 positions. tree_mask[r, t, u] is 1 exactly when draft token u is t or an ancestor of t in request r's tree; every token's parent has a lower index and token 0 is the root. Row a of accept[r] is the one-hot of the token at depth a on one path from the root of request r's tree; the path is longer than 8 tokens. `routing`: each row names 8 different experts; in each aligned block of 64 rows no expert is named by more than 12 rows.
All inputs are finite; a program needn't handle non-finite values.
Results may differ from the reference program's by a relative error of at most 0.014.
Values may be sent and summed in bfloat16 or wider, within the bound.
A program may use at most 128 MiB of HBM per device.

```python
import math
import jax
import jax.numpy as jnp
import numpy as np
from jax import lax

D = 2048
HEADS = 32
KVH = 4
HD = 128
FF = 768
TOP = 8
TREE = 64
CACHE = 4096
ACC = 8
R_DEV = 1
REQUESTS = 8
TOKENS = 512
EXPERTS = 64
QKV = 5120
MOST = 12
N_GX = 8


def tree_parents(key):
    offsets = jax.random.randint(jax.random.fold_in(key, 7), (REQUESTS, TREE), 1, 4)
    parents = jnp.maximum(jnp.arange(TREE, dtype=jnp.int32)[None, :] - offsets, 0)
    return parents.astype(jnp.int32)


def ancestor_mask(parents):
    columns = jnp.arange(TREE, dtype=jnp.int32)

    def climb(step, state):
        marks, nodes = state
        marks = jnp.maximum(marks, (nodes[:, :, None] == columns[None, None, :]).astype(jnp.int32))
        nodes = jnp.take_along_axis(parents, nodes, axis=1)
        return (marks, nodes)
    start_nodes = jnp.broadcast_to(columns[None, :], (REQUESTS, TREE))
    return lax.fori_loop(0, TREE, climb, (jnp.zeros((REQUESTS, TREE, TREE), jnp.int32), start_nodes))[0]


def draw_tree_mask(key, part):
    return ancestor_mask(tree_parents(key))


def draw_accept(key, part):
    marks = ancestor_mask(tree_parents(key))
    leaves = TREE - 1 - jax.random.randint(jax.random.fold_in(key, 11), (REQUESTS,), 0, TREE // 8 + 1)
    path_row = jnp.take_along_axis(marks, leaves[:, None, None], axis=1)[:, 0, :]
    order = jnp.cumsum(path_row, 1)
    wanted = jnp.arange(ACC, dtype=jnp.int32)[None, :, None] + 1
    onehot = (path_row[:, None, :] == 1) & (order[:, None, :] == wanted)
    return onehot.astype(jnp.int32)


def draw_cache_len(key, part):
    lengths = jax.random.randint(jax.random.fold_in(key, 3), (REQUESTS,), CACHE // 16, CACHE + 1)
    longest = jax.random.randint(jax.random.fold_in(key, 5), (), 0, REQUESTS)
    return jnp.where(jnp.arange(REQUESTS) == longest, CACHE, lengths).astype(jnp.int32)


def draw_cache_k(key, part):
    shape = (REQUESTS, CACHE, KVH * HD)
    values = jax.random.truncated_normal(jax.random.fold_in(key, 26), -6.0, 6.0, shape, jnp.float32)
    return values.astype(jnp.bfloat16)


def shard_levels(key, dims, shards, smallest, largest):
    level = 1.0
    for axis_at, blocks in shards:
        draws = jax.random.uniform(jax.random.fold_in(jax.random.fold_in(key, 6), axis_at), (blocks,), jnp.float32, smallest / len(shards), largest / len(shards))
        level = level * jnp.repeat(jnp.exp(draws), dims[axis_at] // blocks).reshape((-1,) + (1,) * (len(dims) - 1 - axis_at))
    return level


def routed_block(stream_key, own, number, rows, number_of, top, bound, lean):
    ranking = jax.random.permutation(stream_key, number_of)
    crowded, ordinary = portions_of(number_of, rows * top, bound, lean, True), portions_of(number_of, rows * top, bound, lean, False)
    places = jnp.arange(number_of)

    def named(sizes, turn):
        used = int((sizes > 0).sum())
        fixed = max(1, used // 4)
        passed = fixed + (places - fixed + turn * (used - fixed)) % max(1, number_of - fixed)
        return jnp.zeros((number_of,), jnp.int32).at[ranking[jnp.where(places < fixed, places, passed)]].set(jnp.asarray(sizes, jnp.int32))

    sizes = jnp.where(number % 4 == 0, named(crowded, number // 4), named(ordinary, number - number // 4 - 1))
    mixed = jax.random.permutation(jax.random.fold_in(own, 3), number_of)
    giver, sink = mixed[0:number_of // 2 * 2:2], mixed[1:number_of // 2 * 2:2]
    room = jnp.minimum(sizes[giver] - 1, bound - sizes[sink]) // 2
    room = jnp.where((giver == ranking[0]) | (sink == ranking[0]) | (sizes[sink] == 0), 0, jnp.maximum(room, 0))
    passed = jax.random.randint(jax.random.fold_in(own, 4), (number_of // 2,), 0, 1 << 20) % (room + 1)
    sizes = sizes.at[giver].add(-passed).at[sink].add(passed)
    members = jnp.searchsorted(jnp.cumsum(sizes), jnp.arange(rows * top), side="right").astype(jnp.int32)
    listing = members.reshape(top, rows).T
    listing = listing[jax.random.permutation(jax.random.fold_in(own, 1), rows)]
    turn = jax.random.randint(jax.random.fold_in(own, 2), (rows, 1), 0, top)
    return jnp.take_along_axis(listing, (jnp.arange(top)[None, :] + turn) % top, axis=1)


def portions_of(count, total, most, slope, full):
    weights = [(1 << 20) // math.isqrt(rank ** slope) + 1 for rank in range(1, count + 1)]
    largest = most if full else min(most, max(-(-total // count), total * weights[0] // sum(weights)))
    least = 1 if total - largest >= count - 1 else 0
    given, surplus = [largest] + [least] * (count - 1), total - largest - least * (count - 1)
    while surplus > 0:
        movable = [i for i in range(1, count) if given[i] < largest] or [i for i in range(1, count) if given[i] < most]
        pool, budget = sum([weights[i] for i in movable]), surplus
        for i in movable:
            addition = min(most - given[i], max(1, budget * weights[i] // pool), surplus)
            given[i] = given[i] + addition
            surplus = surplus - addition
    return np.array(given)


def bell_draw(rng, shape, scale, limit, split=(), held_as=jnp.bfloat16):
    entries = scale * jax.random.normal(rng, shape, jnp.float32)
    if split:
        entries = entries * shard_levels(rng, shape, split, -0.22, 0.18)
    return jnp.clip(entries, -limit, limit).astype(held_as)


def setup_inputs(seed: int = 0) -> dict:
    splits = jax.random.split(jax.random.key(seed), 17)
    states = bell_draw(splits[0], (TOKENS, D), 1.0, 6.0, ((0, 8),))
    attn_gain = jnp.clip(1.0 + 0.18 * jax.random.normal(splits[1], (D,), jnp.float32), 0.099609375, 1.8984375).astype(jnp.bfloat16)
    w_qkv = bell_draw(splits[2], (D, QKV), D ** -0.5, 0.125, ((1, 4),))
    q_gain = jnp.clip(1.0 + 0.18 * jax.random.normal(splits[3], (HD,), jnp.float32), 0.099609375, 1.8984375).astype(jnp.bfloat16)
    k_gain = jnp.clip(1.0 + 0.18 * jax.random.normal(splits[4], (HD,), jnp.float32), 0.099609375, 1.8984375).astype(jnp.bfloat16)
    cache_k = draw_cache_k(jax.random.fold_in(splits[16], 71), 0)
    cache_v = bell_draw(splits[6], (REQUESTS, CACHE, KVH * HD), 1.0, 6.0, ((0, 8), (1, 4)))
    cache_len = draw_cache_len(jax.random.fold_in(splits[16], 71), 0)
    tree_mask = draw_tree_mask(jax.random.fold_in(splits[16], 71), 0)
    w_o = bell_draw(splits[9], (HEADS * HD, D), (HEADS * HD) ** -0.5, 0.09375, ((1, 4),))
    ffn_gain = jnp.clip(1.0 + 0.18 * jax.random.normal(splits[10], (D,), jnp.float32), 0.099609375, 1.8984375).astype(jnp.bfloat16)
    routing_keys = jax.random.split(jax.random.fold_in(splits[11], 1), TOKENS // (R_DEV * TREE))
    routing_turns = jax.random.permutation(jax.random.fold_in(splits[11], 3), TOKENS // (R_DEV * TREE))
    routing = jax.vmap(lambda own, number: routed_block(jax.random.fold_in(splits[11], 2), own, number, R_DEV * TREE, EXPERTS, TOP, MOST, 2))(routing_keys, routing_turns).reshape((TOKENS, TOP))
    route_weight = jnp.clip(jnp.exp(jax.random.uniform(splits[12], (TOKENS, TOP), jnp.float32, math.log(0.05), math.log(0.5))), 0.05, 0.5)
    w_in = bell_draw(splits[13], (EXPERTS, D, 2 * FF), D ** -0.5, 0.125, ((0, 8), (1, 4)))
    w_down = bell_draw(splits[14], (EXPERTS, FF, D), FF ** -0.5, 0.21875, ((0, 8), (2, 4)))
    accept = draw_accept(jax.random.fold_in(splits[16], 71), 0)
    return dict(states=states, attn_gain=attn_gain, w_qkv=w_qkv, q_gain=q_gain, k_gain=k_gain, cache_k=cache_k, cache_v=cache_v, cache_len=cache_len, tree_mask=tree_mask, w_o=w_o, ffn_gain=ffn_gain, routing=routing, route_weight=route_weight, w_in=w_in, w_down=w_down, accept=accept)


EPS = 1e-06
NEG = -1e+30
THETA_LOG = math.log(1000000.0)

def rms_scale(values, gain):
    return values * lax.rsqrt(lax.optimization_barrier(jnp.mean(values * values, -1, keepdims=True)) + EPS) * gain

def rotate(values, position):
    half = values.shape[-1] // 2
    freqs = jnp.exp(jnp.arange(half, dtype=jnp.float32) * (-2.0 * THETA_LOG / values.shape[-1]))
    angles = position.astype(jnp.float32)[..., None] * freqs
    cosine = jnp.cos(angles)
    sine = jnp.sin(angles)
    lower = values[..., :half]
    upper = values[..., half:]
    return jnp.concatenate([lower * cosine - upper * sine, upper * cosine + lower * sine], -1)

def reference(states, attn_gain, w_qkv, q_gain, k_gain, cache_k, cache_v, cache_len, tree_mask, w_o, ffn_gain, routing, route_weight, w_in, w_down, accept):
    group = HEADS // KVH
    normed = rms_scale(states.astype(jnp.float32), attn_gain.astype(jnp.float32)).astype(jnp.bfloat16)
    qkv = jnp.dot(normed, w_qkv, preferred_element_type=jnp.float32).astype(jnp.bfloat16)
    query = qkv[:, :HEADS * HD].reshape(REQUESTS, TREE, KVH, group, HD)
    keys_new = qkv[:, HEADS * HD:HEADS * HD + KVH * HD].reshape(REQUESTS, TREE, KVH, HD)
    values_new = qkv[:, HEADS * HD + KVH * HD:].reshape(REQUESTS, TREE, KVH, HD)
    depth = lax.optimization_barrier(jnp.sum(tree_mask, -1)) - 1
    position = cache_len[:, None] + depth
    q_rot = rotate(rms_scale(query.astype(jnp.float32), q_gain.astype(jnp.float32)), position[:, :, None, None]).astype(jnp.bfloat16)
    k_rot = rotate(rms_scale(keys_new.astype(jnp.float32), k_gain.astype(jnp.float32)), position[:, :, None]).astype(jnp.bfloat16)
    cached_keys = cache_k.reshape(REQUESTS, CACHE, KVH, HD)
    cached_values = cache_v.reshape(REQUESTS, CACHE, KVH, HD)
    score_scale = HD ** (-0.5)

    def one_request(items):
        q_one, k_one, v_one, ck_one, cv_one, length, mask_one = items
        q_float = q_one.astype(jnp.float32)
        scores_cache = jnp.einsum('tkgd,skd->tkgs', q_float, ck_one.astype(jnp.float32)) * score_scale
        scores_tree = jnp.einsum('tkgd,ukd->tkgu', q_float, k_one.astype(jnp.float32)) * score_scale
        valid = (jnp.arange(CACHE) < length)[None, None, None, :]
        tree_ok = (mask_one == 1)[:, None, None, :]
        scores_cache = jnp.where(valid, scores_cache, NEG)
        scores_tree = jnp.where(tree_ok, scores_tree, NEG)
        row_max = jnp.maximum(lax.optimization_barrier(jnp.max(scores_cache, -1)), lax.optimization_barrier(jnp.max(scores_tree, -1)))
        probs_cache = jnp.where(valid, jnp.exp(scores_cache - row_max[..., None]), 0.0).astype(jnp.bfloat16)
        probs_tree = jnp.where(tree_ok, jnp.exp(scores_tree - row_max[..., None]), 0.0).astype(jnp.bfloat16)
        denom_sum = lax.optimization_barrier(jnp.sum(probs_cache.astype(jnp.float32), -1)) + lax.optimization_barrier(jnp.sum(probs_tree.astype(jnp.float32), -1))
        weighted = jnp.einsum('tkgs,skd->tkgd', probs_cache.astype(jnp.float32), cv_one.astype(jnp.float32))
        weighted = weighted + jnp.einsum('tkgu,ukd->tkgd', probs_tree.astype(jnp.float32), v_one.astype(jnp.float32))
        return (weighted / denom_sum[..., None]).astype(jnp.bfloat16).reshape(TREE, HEADS * HD)
    attn = lax.map(one_request, (q_rot, k_rot, values_new, cached_keys, cached_values, cache_len, tree_mask))
    attn = attn.reshape(TOKENS, HEADS * HD)
    resid = (states.astype(jnp.float32) + jnp.dot(attn, w_o, preferred_element_type=jnp.float32)).astype(jnp.bfloat16)
    resid_float = resid.astype(jnp.float32)
    inverse = lax.rsqrt(lax.optimization_barrier(jnp.mean(resid_float * resid_float, -1)) + EPS)
    scaled = (resid_float * ffn_gain.astype(jnp.float32)).astype(jnp.bfloat16)
    padded = jnp.concatenate([scaled, jnp.zeros((1, D), jnp.bfloat16)], 0)
    inverse_pad = jnp.concatenate([inverse, jnp.zeros((1,), jnp.float32)], 0)

    def one_expert(moe_sum, expert_id):
        matched = routing == expert_id
        weight_col = lax.optimization_barrier(jnp.sum(jnp.where(matched, route_weight, 0.0), -1))
        weight_pad = jnp.concatenate([weight_col, jnp.zeros((1,), jnp.float32)], 0)
        slot_idx = jnp.nonzero(jnp.any(matched, -1), size=N_GX * MOST, fill_value=TOKENS)[0].astype(jnp.int32)
        gate_up = jnp.dot(padded[slot_idx], w_in[expert_id], preferred_element_type=jnp.float32)
        row_scale = inverse_pad[slot_idx][:, None]
        hidden = (jax.nn.silu(gate_up[:, :FF] * row_scale) * (gate_up[:, FF:] * row_scale)).astype(jnp.bfloat16)
        out_rows = jnp.dot(hidden, w_down[expert_id], preferred_element_type=jnp.float32)
        return (moe_sum.at[slot_idx].add(out_rows * weight_pad[slot_idx][:, None], mode='drop'), None)
    moe_total = lax.scan(one_expert, jnp.zeros((TOKENS, D), jnp.float32), jnp.arange(EXPERTS, dtype=jnp.int32))[0]
    layer_out = (resid_float + moe_total).astype(jnp.bfloat16)
    kv_new = jnp.concatenate([k_rot.reshape(REQUESTS, TREE, KVH * HD), values_new.reshape(REQUESTS, TREE, KVH * HD)], -1)
    accepted_kv = jnp.einsum('rat,rtc->rac', accept.astype(jnp.float32), kv_new.astype(jnp.float32)).astype(jnp.bfloat16)
    return (layer_out, accepted_kv)
```

```python
import math

import jax
import jax.numpy as jnp
from jax import lax
from jax.experimental import pallas as pl
from jax.experimental.pallas import tpu as pltpu
from jax.sharding import PartitionSpec as P

EPS = 1e-06
NEG = -1e30
THETA_LOG = math.log(1000000.0)


MESH = pl.DeviceIdType.MESH


def exchange(arrays, axis, scatter, cid):
    count = lax.axis_size(axis)
    number = len(arrays)

    def kernel(*refs):
        ins, outs = refs[:number], refs[number : 2 * number]
        send, recv, local = refs[2 * number :]
        me = lax.axis_index(axis)
        barrier = pltpu.get_barrier_semaphore()
        for d in range(1, count):
            pl.semaphore_signal(
                barrier, inc=1, device_id={axis: lax.rem(me + d, count)}, device_id_type=MESH
            )
        pl.semaphore_wait(barrier, count - 1)
        copies = []
        for d in range(1, count):
            peer = lax.rem(me + d, count)
            for i in range(number):
                copy = pltpu.make_async_remote_copy(
                    src_ref=ins[i].at[peer] if scatter else ins[i],
                    dst_ref=outs[i].at[me],
                    send_sem=send.at[i, d],
                    recv_sem=recv.at[i, d],
                    device_id={axis: peer},
                    device_id_type=MESH,
                )
                copy.start()
                copies.append(copy)
        own = []
        for i in range(number):
            copy = pltpu.make_async_copy(
                ins[i].at[me] if scatter else ins[i], outs[i].at[me], local.at[i]
            )
            copy.start()
            own.append(copy)
        for copy in own + copies:
            copy.wait()

    outs = [
        jax.ShapeDtypeStruct(x.shape if scatter else (count,) + x.shape, x.dtype) for x in arrays
    ]
    return pl.pallas_call(
        kernel,
        out_shape=outs,
        in_specs=[pl.BlockSpec(memory_space=pltpu.VMEM)] * number,
        out_specs=[pl.BlockSpec(memory_space=pltpu.VMEM)] * number,
        scratch_shapes=[
            pltpu.SemaphoreType.DMA((number, count)),
            pltpu.SemaphoreType.DMA((number, count)),
            pltpu.SemaphoreType.DMA((number,)),
        ],
        compiler_params=pltpu.CompilerParams(collective_id=cid, has_side_effects=True),
        name="exchange_%d" % cid,
    )(*arrays)


def expert_hidden(rows, squares, w_in, model_width, cid):
    axis = "gy"
    count = lax.axis_size(axis)
    experts, slots, depth = rows.shape
    wide = w_in.shape[2]
    units = wide // 2
    half = experts // 2
    sub = 2
    piece = slots // sub
    chunks = half * sub
    lag = 2

    def kernel(
        x_ref, sq_ref, w_hbm, hid_ref, wbuf, part, rbuf, sqbuf, inv_ref,
        wsem, rs_s, rs_r, h_s, h_r, sq_s, sq_r,
    ):
        me = lax.axis_index(axis)
        prev = lax.rem(me + count - 1, count)
        nxt = lax.rem(me + 1, count)
        at_low = me == 0
        at_high = me == count - 1

        def load(e):
            return pltpu.make_async_copy(w_hbm.at[e], wbuf.at[e], wsem.at[e])

        for s in range(half):
            load(half + s).start()
            load(s).start()
        barrier = pltpu.get_barrier_semaphore()
        for d in range(1, count):
            pl.semaphore_signal(
                barrier, inc=1, device_id={axis: lax.rem(me + d, count)}, device_id_type=MESH
            )
        pl.semaphore_wait(barrier, count - 1)

        def sq_copy(d):
            return pltpu.make_async_remote_copy(
                src_ref=sq_ref,
                dst_ref=sqbuf.at[d],
                send_sem=sq_s.at[d],
                recv_sem=sq_r.at[d],
                device_id={axis: lax.rem(me + d, count)},
                device_id_type=MESH,
            )

        for d in range(1, count):
            sq_copy(d).start()
        total = sq_ref[...]
        for d in range(1, count):
            sq_copy(d).wait()
            total = total + sqbuf[d]
        inv_ref[...] = lax.rsqrt(total / model_width + EPS)
        diagonal = lax.broadcasted_iota(jnp.int32, (piece, 128), 0) == lax.broadcasted_iota(
            jnp.int32, (piece, 128), 1
        )

        def rs_copy(h, c):
            return pltpu.make_async_remote_copy(
                src_ref=part.at[h, c],
                dst_ref=rbuf.at[h, c],
                send_sem=rs_s.at[h, c],
                recv_sem=rs_r.at[h, c],
                device_id={axis: nxt if h else prev},
                device_id_type=MESH,
            )

        def hid_copy(h, c):
            return pltpu.make_async_remote_copy(
                src_ref=hid_ref.at[h, c],
                dst_ref=hid_ref.at[h, c],
                send_sem=h_s.at[h, c],
                recv_sem=h_r.at[h, c],
                device_id={axis: prev if h else nxt},
                device_id_type=MESH,
            )

        def ends(h):
            return (at_low, at_high) if h else (at_high, at_low)

        def reduce_chunk(h, c):
            first, last = ends(h)

            @pl.when(jnp.logical_not(first))
            def _():
                rs_copy(h, c).wait_recv()

            @pl.when(jnp.logical_not(jnp.logical_or(first, last)))
            def _():
                part[h, c] = (
                    part[h, c].astype(jnp.float32) + rbuf[h, c].astype(jnp.float32)
                ).astype(jnp.bfloat16)

            @pl.when(jnp.logical_not(last))
            def _():
                rs_copy(h, c).start()

            @pl.when(last)
            def _():
                row = inv_ref[pl.ds(h * chunks + c, 1), :]
                inverse = jnp.sum(jnp.where(diagonal, row, 0.0), 1, keepdims=True)
                summed = part[h, c].astype(jnp.float32) + rbuf[h, c].astype(jnp.float32)
                gate = summed[:, :units] * inverse
                up = summed[:, units:] * inverse
                hid_ref[h, c] = (gate / (1.0 + jnp.exp(-gate)) * up).astype(jnp.bfloat16)
                hid_copy(h, c).start()

        def return_chunk(h, c):
            first, last = ends(h)

            @pl.when(jnp.logical_not(last))
            def _():
                hid_copy(h, c).wait_recv()

            @pl.when(jnp.logical_not(jnp.logical_or(first, last)))
            def _():
                hid_copy(h, c).start()

        def step(s, carry):
            @pl.when(s < half)
            def _():
                for h in (1, 0):
                    e = h * half + s
                    load(e).wait()
                    value = jnp.dot(x_ref[e], wbuf[e], preferred_element_type=jnp.float32)
                    for j in range(sub):
                        part[h, s * sub + j] = value[j * piece : (j + 1) * piece].astype(
                            jnp.bfloat16
                        )
                for j in range(sub):
                    for h in (1, 0):
                        reduce_chunk(h, s * sub + j)

            @pl.when(s >= lag)
            def _():
                for j in range(sub):
                    for h in (1, 0):
                        return_chunk(h, (s - lag) * sub + j)

            return carry

        lax.fori_loop(0, half + lag, step, 0)

        def finish(c, carry):
            for h in (1, 0):
                first, last = ends(h)

                @pl.when(jnp.logical_not(last))
                def _():
                    rs_copy(h, c).wait_send()

                @pl.when(jnp.logical_not(first))
                def _():
                    hid_copy(h, c).wait_send()

            return carry

        lax.fori_loop(0, chunks, finish, 0)

    hidden = pl.pallas_call(
        kernel,
        out_shape=jax.ShapeDtypeStruct((2, chunks, piece, units), jnp.bfloat16),
        in_specs=[
            pl.BlockSpec(memory_space=pltpu.VMEM),
            pl.BlockSpec(memory_space=pltpu.VMEM),
            pl.BlockSpec(memory_space=pl.ANY),
        ],
        out_specs=pl.BlockSpec(memory_space=pltpu.VMEM),
        scratch_shapes=[
            pltpu.VMEM((experts, depth, wide), jnp.bfloat16),
            pltpu.VMEM((2, chunks, piece, wide), jnp.bfloat16),
            pltpu.VMEM((2, chunks, piece, wide), jnp.bfloat16),
            pltpu.VMEM((count, 2 * chunks, 128), jnp.float32),
            pltpu.VMEM((2 * chunks, 128), jnp.float32),
            pltpu.SemaphoreType.DMA((experts,)),
            pltpu.SemaphoreType.DMA((2, chunks)),
            pltpu.SemaphoreType.DMA((2, chunks)),
            pltpu.SemaphoreType.DMA((2, chunks)),
            pltpu.SemaphoreType.DMA((2, chunks)),
            pltpu.SemaphoreType.DMA((count,)),
            pltpu.SemaphoreType.DMA((count,)),
        ],
        compiler_params=pltpu.CompilerParams(
            collective_id=cid, has_side_effects=True, vmem_limit_bytes=48 * 1024 * 1024
        ),
        name="expert_hidden",
    )(rows, squares, w_in)
    return hidden.reshape(experts, slots, units)


def rms_scale(values, gain):
    return values * lax.rsqrt(jnp.mean(values * values, -1, keepdims=True) + EPS) * gain


def rotate(values, position):
    half = values.shape[-1] // 2
    freqs = jnp.exp(jnp.arange(half, dtype=jnp.float32) * (-2.0 * THETA_LOG / values.shape[-1]))
    angles = position.astype(jnp.float32)[..., None] * freqs
    cosine = jnp.cos(angles)
    sine = jnp.sin(angles)
    lower = values[..., :half]
    upper = values[..., half:]
    return jnp.concatenate([lower * cosine - upper * sine, upper * cosine + lower * sine], -1)


def body(
    states,
    attn_gain,
    w_qkv,
    q_gain,
    k_gain,
    cache_k,
    cache_v,
    cache_len,
    tree_mask,
    w_o,
    ffn_gain,
    routing,
    route_weight,
    w_in,
    w_down,
    accept,
):
    tok_rows, model_width = states.shape
    head_dim = q_gain.shape[0]
    kv_cols = cache_k.shape[2]
    kv_heads = kv_cols // head_dim
    heads_all = w_o.shape[0] // head_dim
    group = heads_all // kv_heads
    requests_here, tree_size = (tree_mask.shape[0], tree_mask.shape[1])
    cache_span = cache_k.shape[1]
    cols_here = w_o.shape[1]
    col_index = lax.axis_index("gy")
    row_index = lax.axis_index("gx")
    count_gx = lax.axis_size("gx")
    normed = rms_scale(states.astype(jnp.float32), attn_gain.astype(jnp.float32)).astype(
        jnp.bfloat16
    )
    qkv_part = jnp.dot(normed, w_qkv, preferred_element_type=jnp.float32).astype(jnp.bfloat16)
    (qkv_blocks,) = exchange([qkv_part], "gy", False, 0)
    qkv_whole = jnp.swapaxes(qkv_blocks, 0, 1).reshape(tok_rows, -1)
    q_cols = heads_all * head_dim
    query = qkv_whole[:, :q_cols].reshape(requests_here, tree_size, kv_heads, group, head_dim)
    keys_new = qkv_whole[:, q_cols : q_cols + kv_cols].reshape(
        requests_here, tree_size, kv_heads, head_dim
    )
    values_new = qkv_whole[:, q_cols + kv_cols :].reshape(
        requests_here, tree_size, kv_heads, head_dim
    )
    depth = jnp.sum(tree_mask, -1) - 1
    position = cache_len[:, None] + depth
    q_rot = rotate(
        rms_scale(query.astype(jnp.float32), q_gain.astype(jnp.float32)), position[:, :, None, None]
    ).astype(jnp.bfloat16)
    k_rot = rotate(
        rms_scale(keys_new.astype(jnp.float32), k_gain.astype(jnp.float32)), position[:, :, None]
    ).astype(jnp.bfloat16)
    cached_keys = cache_k.reshape(requests_here, cache_span, kv_heads, head_dim)
    cached_values = cache_v.reshape(requests_here, cache_span, kv_heads, head_dim)
    score_scale = head_dim ** (-0.5)
    scores_cache = (
        jnp.einsum("rtkgd,rskd->rtkgs", q_rot, cached_keys, preferred_element_type=jnp.float32)
        * score_scale
    )
    scores_tree = (
        jnp.einsum("rtkgd,rukd->rtkgu", q_rot, k_rot, preferred_element_type=jnp.float32)
        * score_scale
    )
    cache_pos = col_index * cache_span + jnp.arange(cache_span, dtype=jnp.int32)
    valid = (cache_pos[None, :] < cache_len[:, None])[:, None, None, None, :]
    tree_ok = ((tree_mask == 1) & (col_index == 0))[:, :, None, None, :]
    scores_cache = jnp.where(valid, scores_cache, NEG)
    scores_tree = jnp.where(tree_ok, scores_tree, NEG)
    row_max = jnp.maximum(jnp.max(scores_cache, -1), jnp.max(scores_tree, -1))
    probs_cache = jnp.where(valid, jnp.exp(scores_cache - row_max[..., None]), 0.0).astype(
        jnp.bfloat16
    )
    probs_tree = jnp.where(tree_ok, jnp.exp(scores_tree - row_max[..., None]), 0.0).astype(
        jnp.bfloat16
    )
    denom_sum = jnp.sum(probs_cache.astype(jnp.float32), -1) + jnp.sum(
        probs_tree.astype(jnp.float32), -1
    )
    weighted = jnp.einsum(
        "rtkgs,rskd->rtkgd", probs_cache, cached_values, preferred_element_type=jnp.float32
    )
    weighted = weighted + jnp.einsum(
        "rtkgu,rukd->rtkgd", probs_tree, values_new, preferred_element_type=jnp.float32
    )
    count_gy = lax.axis_size("gy")
    heads_here = heads_all // count_gy
    blocks = jnp.swapaxes(
        weighted.astype(jnp.bfloat16).reshape(tok_rows, count_gy, heads_here * head_dim), 0, 1
    )
    stats = jnp.stack([row_max, denom_sum]).reshape(2, tok_rows, count_gy, heads_here)
    stats = stats.transpose(2, 0, 1, 3).reshape(count_gy, -1, 128)
    blocks, stats = exchange([blocks, stats], "gy", True, 1)
    stats = stats.reshape(count_gy, 2, tok_rows, heads_here)
    factor = jnp.exp(stats[:, 0] - jnp.max(stats[:, 0], 0))
    denom = jnp.sum(stats[:, 1] * factor, 0)
    factor = factor / denom
    attn_part = jnp.sum(
        blocks.astype(jnp.float32).reshape(count_gy, tok_rows, heads_here, head_dim)
        * factor[..., None],
        0,
    )
    attn_part = attn_part.astype(jnp.bfloat16).reshape(tok_rows, heads_here * head_dim)
    (attn,) = exchange([attn_part], "gy", False, 2)
    attn = jnp.swapaxes(attn, 0, 1).reshape(tok_rows, q_cols)
    states_here = lax.dynamic_slice_in_dim(states, col_index * cols_here, cols_here, 1)
    resid = (
        states_here.astype(jnp.float32) + jnp.dot(attn, w_o, preferred_element_type=jnp.float32)
    ).astype(jnp.bfloat16)
    exp_here = w_in.shape[0]
    expert_count = exp_here * count_gx
    top_k = routing.shape[1]
    most_rows = 3 * tok_rows * top_k // (2 * expert_count)
    hidden_units = w_down.shape[1]
    gain_float = ffn_gain.astype(jnp.float32)
    tokens = routing.shape[0]
    slots = count_gx * most_rows
    own_experts = row_index * exp_here + jnp.arange(exp_here, dtype=jnp.int32)
    matched = routing[:, None, :] == own_experts[None, :, None]
    hits = jnp.any(matched, -1)
    weights = jnp.sum(jnp.where(matched, route_weight[:, None, :], 0.0), -1)
    order = jnp.arange(tok_rows, dtype=jnp.int32)
    earlier = (order[:, None] > order[None, :]).astype(jnp.bfloat16)
    rank = jnp.einsum(
        "tu,bue->bte",
        earlier,
        hits.astype(jnp.bfloat16).reshape(count_gx, tok_rows, exp_here),
        preferred_element_type=jnp.float32,
    ).astype(jnp.int32)
    first_slot = jnp.arange(count_gx, dtype=jnp.int32)[:, None, None] * most_rows
    slot_of = jnp.where(hits, (rank + first_slot).reshape(tokens, exp_here), -1)
    pick = slot_of.T[:, None, :] == jnp.arange(slots, dtype=jnp.int32)[None, :, None]
    pick_matrix = pick.astype(jnp.bfloat16)
    slot_weight = jnp.sum(jnp.where(pick, weights.T[:, None, :], 0.0), -1)
    (gathered,) = exchange([resid], "gx", False, 3)
    gathered = gathered.reshape(tokens, cols_here).astype(jnp.float32)
    token_squares = jnp.sum(gathered * gathered, -1)
    slot_squares = jnp.sum(jnp.where(pick, token_squares, 0.0), -1)
    piece = slots // 2
    slot_squares = jnp.pad(slot_squares.reshape(-1, piece), ((0, 0), (0, 128 - piece)))
    scaled = (gathered * gain_float).astype(jnp.bfloat16)
    rows = jnp.einsum(
        "est,td->esd", pick_matrix, scaled, preferred_element_type=jnp.float32
    ).astype(jnp.bfloat16)
    hidden = expert_hidden(rows, slot_squares, w_in, model_width, 4)
    expert_out = jnp.einsum("esf,efd->esd", hidden, w_down, preferred_element_type=jnp.float32)
    expert_out = (expert_out * slot_weight[..., None]).astype(jnp.bfloat16)
    partial_moe = jnp.einsum(
        "est,esd->td", pick_matrix, expert_out, preferred_element_type=jnp.float32
    ).astype(jnp.bfloat16)
    (returned,) = exchange(
        [partial_moe.reshape(count_gx, tok_rows, cols_here)], "gx", True, 5
    )
    moe_total = jnp.sum(returned.astype(jnp.float32), 0)
    layer_out = (resid.astype(jnp.float32) + moe_total).astype(jnp.bfloat16)
    kv_new = jnp.concatenate(
        [
            k_rot.reshape(requests_here, tree_size, kv_cols),
            values_new.reshape(requests_here, tree_size, kv_cols),
        ],
        -1,
    )
    accepted_kv = jnp.einsum(
        "rat,rtc->rac", accept.astype(jnp.bfloat16), kv_new, preferred_element_type=jnp.float32
    ).astype(jnp.bfloat16)
    return (layer_out, accepted_kv)


def solution(mesh):
    in_specs = (
        P("gx", None),
        P(),
        P(None, "gy"),
        P(),
        P(),
        P("gx", "gy", None),
        P("gx", "gy", None),
        P("gx"),
        P("gx", None, None),
        P(None, "gy"),
        P("gy"),
        P(),
        P(),
        P("gx", "gy", None),
        P("gx", None, "gy"),
        P("gx", None, None),
    )
    out_specs = (P("gx", "gy"), P("gx", None, None))
    return jax.shard_map(body, mesh=mesh, in_specs=in_specs, out_specs=out_specs, check_vma=False)
```

```python
import math

import jax
import jax.numpy as jnp
from jax import lax
from jax.experimental import pallas as pl
from jax.experimental.pallas import tpu as pltpu
from jax.sharding import PartitionSpec as P

EPS = 1e-06
NEG = -1e30
THETA_LOG = math.log(1000000.0)


MESH = pl.DeviceIdType.MESH


def exchange(arrays, axis, scatter, cid):
    count = lax.axis_size(axis)
    number = len(arrays)

    def kernel(*refs):
        ins, outs = refs[:number], refs[number : 2 * number]
        send, recv, local = refs[2 * number :]
        me = lax.axis_index(axis)
        barrier = pltpu.get_barrier_semaphore()
        for d in range(1, count):
            pl.semaphore_signal(
                barrier, inc=1, device_id={axis: lax.rem(me + d, count)}, device_id_type=MESH
            )
        pl.semaphore_wait(barrier, count - 1)
        copies = []
        for d in range(1, count):
            peer = lax.rem(me + d, count)
            for i in range(number):
                copy = pltpu.make_async_remote_copy(
                    src_ref=ins[i].at[peer] if scatter else ins[i],
                    dst_ref=outs[i].at[me],
                    send_sem=send.at[i, d],
                    recv_sem=recv.at[i, d],
                    device_id={axis: peer},
                    device_id_type=MESH,
                )
                copy.start()
                copies.append(copy)
        own = []
        for i in range(number):
            copy = pltpu.make_async_copy(
                ins[i].at[me] if scatter else ins[i], outs[i].at[me], local.at[i]
            )
            copy.start()
            own.append(copy)
        for copy in own + copies:
            copy.wait()

    outs = [
        jax.ShapeDtypeStruct(x.shape if scatter else (count,) + x.shape, x.dtype) for x in arrays
    ]
    return pl.pallas_call(
        kernel,
        out_shape=outs,
        in_specs=[pl.BlockSpec(memory_space=pltpu.VMEM)] * number,
        out_specs=[pl.BlockSpec(memory_space=pltpu.VMEM)] * number,
        scratch_shapes=[
            pltpu.SemaphoreType.DMA((number, count)),
            pltpu.SemaphoreType.DMA((number, count)),
            pltpu.SemaphoreType.DMA((number,)),
        ],
        compiler_params=pltpu.CompilerParams(collective_id=cid, has_side_effects=True),
        name="exchange_%d" % cid,
    )(*arrays)


def expert_hidden(rows, squares, w_in, model_width, cid):
    axis = "gy"
    count = lax.axis_size(axis)
    experts, slots, depth = rows.shape
    wide = w_in.shape[2]
    units = wide // 2
    half = experts // 2
    piece = 16
    sub = slots // piece
    chunks = half * sub
    hop = 2
    far = hop * (count - 1)

    def kernel(
        x_ref, sq_ref, w_hbm, hid_ref, wbuf, part, rbuf, sqbuf, inv_ref,
        wsem, rs_s, rs_r, h_s, h_r, sq_s, sq_r,
    ):
        me = lax.axis_index(axis)
        prev = lax.rem(me + count - 1, count)
        nxt = lax.rem(me + 1, count)
        at_low = me == 0
        at_high = me == count - 1

        def load(e):
            return pltpu.make_async_copy(w_hbm.at[e], wbuf.at[e], wsem.at[e])

        for s in range(half):
            load(half + s).start()
            load(s).start()
        barrier = pltpu.get_barrier_semaphore()
        for d in range(1, count):
            pl.semaphore_signal(
                barrier, inc=1, device_id={axis: lax.rem(me + d, count)}, device_id_type=MESH
            )
        pl.semaphore_wait(barrier, count - 1)

        def sq_copy(d):
            return pltpu.make_async_remote_copy(
                src_ref=sq_ref,
                dst_ref=sqbuf.at[d],
                send_sem=sq_s.at[d],
                recv_sem=sq_r.at[d],
                device_id={axis: lax.rem(me + d, count)},
                device_id_type=MESH,
            )

        for d in range(1, count):
            sq_copy(d).start()
        total = sq_ref[...]
        for d in range(1, count):
            sq_copy(d).wait()
            total = total + sqbuf[d]
        inv_ref[...] = lax.rsqrt(total / model_width + EPS)
        diagonal = lax.broadcasted_iota(jnp.int32, (piece, 128), 0) == lax.broadcasted_iota(
            jnp.int32, (piece, 128), 1
        )

        def rs_copy(h, c):
            return pltpu.make_async_remote_copy(
                src_ref=part.at[h, c],
                dst_ref=rbuf.at[h, c],
                send_sem=rs_s.at[h, c],
                recv_sem=rs_r.at[h, c],
                device_id={axis: nxt if h else prev},
                device_id_type=MESH,
            )

        def hid_copy(h, c):
            return pltpu.make_async_remote_copy(
                src_ref=hid_ref.at[h, c],
                dst_ref=hid_ref.at[h, c],
                send_sem=h_s.at[h, c],
                recv_sem=h_r.at[h, c],
                device_id={axis: prev if h else nxt},
                device_id_type=MESH,
            )

        def ends(h):
            return (at_low, at_high) if h else (at_high, at_low)

        def reduce_chunk(h, c):
            first, last = ends(h)

            @pl.when(jnp.logical_not(first))
            def _():
                rs_copy(h, c).wait_recv()

            @pl.when(jnp.logical_not(jnp.logical_or(first, last)))
            def _():
                part[h, c] = (
                    part[h, c].astype(jnp.float32) + rbuf[h, c].astype(jnp.float32)
                ).astype(jnp.bfloat16)

            @pl.when(jnp.logical_not(last))
            def _():
                rs_copy(h, c).start()

            @pl.when(last)
            def _():
                row = inv_ref[pl.ds(h * chunks + c, 1), :]
                inverse = jnp.sum(jnp.where(diagonal, row, 0.0), 1, keepdims=True)
                summed = part[h, c].astype(jnp.float32) + rbuf[h, c].astype(jnp.float32)
                gate = summed[:, :units] * inverse
                up = summed[:, units:] * inverse
                hid_ref[h, c] = (gate / (1.0 + jnp.exp(-gate)) * up).astype(jnp.bfloat16)
                hid_copy(h, c).start()

        def return_chunk(h, c):
            first, last = ends(h)

            @pl.when(jnp.logical_not(last))
            def _():
                hid_copy(h, c).wait_recv()

            @pl.when(jnp.logical_not(jnp.logical_or(first, last)))
            def _():
                hid_copy(h, c).start()

        def multiply(s):
            for h in (1, 0):
                e = h * half + s
                load(e).wait()
                value = jnp.dot(x_ref[e], wbuf[e], preferred_element_type=jnp.float32)
                for j in range(sub):
                    part[h, s * sub + j] = value[j * piece : (j + 1) * piece].astype(jnp.bfloat16)

        def step(t, carry):
            @pl.when(jnp.logical_and(t < chunks, lax.rem(t, sub) == 0))
            def _():
                multiply(lax.div(t, sub))

            for h in (1, 0):
                way = hop * (me if h else count - 1 - me)
                c = t - way

                @pl.when(jnp.logical_and(c >= 0, c < chunks))
                def _():
                    reduce_chunk(h, c)

            for h in (1, 0):
                way = hop * (me if h else count - 1 - me)
                b = t - 2 * far + way

                @pl.when(jnp.logical_and(b >= 0, b < chunks))
                def _():
                    return_chunk(h, b)

            return carry

        lax.fori_loop(0, chunks + 2 * far, step, 0)

        def finish(c, carry):
            for h in (1, 0):
                first, last = ends(h)

                @pl.when(jnp.logical_not(last))
                def _():
                    rs_copy(h, c).wait_send()

                @pl.when(jnp.logical_not(first))
                def _():
                    hid_copy(h, c).wait_send()

            return carry

        lax.fori_loop(0, chunks, finish, 0)

    hidden = pl.pallas_call(
        kernel,
        out_shape=jax.ShapeDtypeStruct((2, chunks, piece, units), jnp.bfloat16),
        in_specs=[
            pl.BlockSpec(memory_space=pltpu.VMEM),
            pl.BlockSpec(memory_space=pltpu.VMEM),
            pl.BlockSpec(memory_space=pl.ANY),
        ],
        out_specs=pl.BlockSpec(memory_space=pltpu.VMEM),
        scratch_shapes=[
            pltpu.VMEM((experts, depth, wide), jnp.bfloat16),
            pltpu.VMEM((2, chunks, piece, wide), jnp.bfloat16),
            pltpu.VMEM((2, chunks, piece, wide), jnp.bfloat16),
            pltpu.VMEM((count, 2 * chunks, 128), jnp.float32),
            pltpu.VMEM((2 * chunks, 128), jnp.float32),
            pltpu.SemaphoreType.DMA((experts,)),
            pltpu.SemaphoreType.DMA((2, chunks)),
            pltpu.SemaphoreType.DMA((2, chunks)),
            pltpu.SemaphoreType.DMA((2, chunks)),
            pltpu.SemaphoreType.DMA((2, chunks)),
            pltpu.SemaphoreType.DMA((count,)),
            pltpu.SemaphoreType.DMA((count,)),
        ],
        compiler_params=pltpu.CompilerParams(
            collective_id=cid, has_side_effects=True, vmem_limit_bytes=48 * 1024 * 1024
        ),
        name="expert_hidden",
    )(rows, squares, w_in)
    return hidden.reshape(experts, slots, units)


def attend(qkv, q_gain, k_gain, cosine, sine, cache_k, cache_v, bounds, tree_mask, blocks):
    tokens = qkv.shape[0]
    span, kv_cols = cache_k.shape
    dim = q_gain.shape[1]
    kv_heads = kv_cols // dim
    heads = qkv.shape[1] // dim - 2 * kv_heads
    group = heads // kv_heads
    per_block = heads // blocks
    blocks_here = blocks // kv_heads
    scale = dim ** (-0.5)

    def kernel(
        bounds_ref, q_ref, kn_ref, vn_ref, qg_ref, kg_ref, cos_ref, sin_ref, k_ref, v_ref,
        mask_ref, acc_ref, stat_ref, rot_ref,
    ):
        cos = cos_ref[...]
        sin = sin_ref[...]

        def turn(value, gain):
            value = value.astype(jnp.float32)
            value = value * lax.rsqrt(jnp.mean(value * value, -1, keepdims=True) + EPS) * gain
            return (value * cos + pltpu.roll(value, dim // 2, 1) * sin).astype(jnp.bfloat16)

        gain = qg_ref[...].astype(jnp.float32)
        query = jnp.concatenate(
            [turn(q_ref[:, i * dim : (i + 1) * dim], gain) for i in range(group)], 0
        )
        keys = turn(kn_ref[...], kg_ref[...].astype(jnp.float32))
        rot_ref[...] = keys
        contract = (((1,), (1,)), ((), ()))
        tree = (
            lax.dot_general(query, keys, contract, preferred_element_type=jnp.float32) * scale
        )
        mask = jnp.concatenate([mask_ref[...]] * group, 0)
        tree_ok = jnp.logical_and(mask == 1, bounds_ref[1] == 0)
        tree = jnp.where(tree_ok, tree, NEG)
        score = (
            lax.dot_general(query, k_ref[...], contract, preferred_element_type=jnp.float32)
            * scale
        )
        valid = lax.broadcasted_iota(jnp.int32, score.shape, 1) < bounds_ref[0]
        score = jnp.where(valid, score, NEG)
        top = jnp.maximum(
            jnp.max(score, 1, keepdims=True), jnp.max(tree, 1, keepdims=True)
        )
        prob = jnp.where(valid, jnp.exp(score - top), 0.0).astype(jnp.bfloat16)
        prob_tree = jnp.where(tree_ok, jnp.exp(tree - top), 0.0).astype(jnp.bfloat16)
        total = jnp.sum(prob.astype(jnp.float32), 1, keepdims=True) + jnp.sum(
            prob_tree.astype(jnp.float32), 1, keepdims=True
        )
        acc = jnp.dot(prob, v_ref[...], preferred_element_type=jnp.float32)
        acc = acc + jnp.dot(prob_tree, vn_ref[...], preferred_element_type=jnp.float32)
        acc = acc.astype(jnp.bfloat16)
        diagonal = lax.broadcasted_iota(jnp.int32, (tokens, 128), 0) == lax.broadcasted_iota(
            jnp.int32, (tokens, 128), 1
        )
        for i in range(group):
            rows = slice(i * tokens, (i + 1) * tokens)
            block, place = divmod(i, per_block)
            acc_ref[block, :, place * dim : (place + 1) * dim] = acc[rows]
            for j, column in enumerate((top, total)):
                stat_ref[block, j * per_block + place : j * per_block + place + 1, :] = jnp.sum(
                    jnp.where(diagonal, column[rows], 0.0), 0, keepdims=True
                )

    whole = lambda shape: pl.BlockSpec(shape, lambda g: (0,) * len(shape))
    return pl.pallas_call(
        kernel,
        grid=(kv_heads,),
        out_shape=[
            jax.ShapeDtypeStruct((blocks, tokens, per_block * dim), jnp.bfloat16),
            jax.ShapeDtypeStruct((blocks, 2 * per_block, 128), jnp.float32),
            jax.ShapeDtypeStruct((tokens, kv_cols), jnp.bfloat16),
        ],
        in_specs=[
            pl.BlockSpec(memory_space=pltpu.SMEM),
            pl.BlockSpec((tokens, group * dim), lambda g: (0, g)),
            pl.BlockSpec((tokens, dim), lambda g: (0, heads + g)),
            pl.BlockSpec((tokens, dim), lambda g: (0, heads + kv_heads + g)),
            whole((1, dim)),
            whole((1, dim)),
            whole((tokens, dim)),
            whole((tokens, dim)),
            pl.BlockSpec((span, dim), lambda g: (0, g)),
            pl.BlockSpec((span, dim), lambda g: (0, g)),
            whole((tokens, tokens)),
        ],
        out_specs=[
            pl.BlockSpec((blocks_here, tokens, per_block * dim), lambda g: (g, 0, 0)),
            pl.BlockSpec((blocks_here, 2 * per_block, 128), lambda g: (g, 0, 0)),
            pl.BlockSpec((tokens, dim), lambda g: (0, g)),
        ],
        compiler_params=pltpu.CompilerParams(vmem_limit_bytes=40 * 1024 * 1024),
        name="attend",
    )(bounds, qkv, qkv, qkv, q_gain, k_gain, cosine, sine, cache_k, cache_v, tree_mask)


def rms_scale(values, gain):
    return values * lax.rsqrt(jnp.mean(values * values, -1, keepdims=True) + EPS) * gain


def angles_of(position, dim):
    freqs = jnp.exp(jnp.arange(dim // 2, dtype=jnp.float32) * (-2.0 * THETA_LOG / dim))
    angles = position.astype(jnp.float32)[..., None] * freqs
    cosine = jnp.cos(angles)
    sine = jnp.sin(angles)
    return jnp.concatenate([cosine, cosine], -1), jnp.concatenate([-sine, sine], -1)


def body(
    states,
    attn_gain,
    w_qkv,
    q_gain,
    k_gain,
    cache_k,
    cache_v,
    cache_len,
    tree_mask,
    w_o,
    ffn_gain,
    routing,
    route_weight,
    w_in,
    w_down,
    accept,
):
    tok_rows, model_width = states.shape
    head_dim = q_gain.shape[0]
    kv_cols = cache_k.shape[2]
    heads_all = w_o.shape[0] // head_dim
    cache_span = cache_k.shape[1]
    cols_here = w_o.shape[1]
    col_index = lax.axis_index("gy")
    row_index = lax.axis_index("gx")
    count_gx = lax.axis_size("gx")
    normed = rms_scale(states.astype(jnp.float32), attn_gain.astype(jnp.float32)).astype(
        jnp.bfloat16
    )
    qkv_part = jnp.dot(normed, w_qkv, preferred_element_type=jnp.float32).astype(jnp.bfloat16)
    (qkv_blocks,) = exchange([qkv_part], "gy", False, 0)
    qkv_whole = jnp.swapaxes(qkv_blocks, 0, 1).reshape(tok_rows, -1)
    q_cols = heads_all * head_dim
    depth = jnp.sum(tree_mask, -1) - 1
    cosine, sine = angles_of((cache_len[:, None] + depth)[0], head_dim)
    bounds = jnp.concatenate([cache_len - col_index * cache_span, col_index[None]])
    count_gy = lax.axis_size("gy")
    heads_here = heads_all // count_gy
    blocks, stats, k_rot = attend(
        qkv_whole,
        q_gain[None],
        k_gain[None],
        cosine,
        sine,
        cache_k[0],
        cache_v[0],
        bounds,
        tree_mask[0],
        count_gy,
    )
    blocks, stats = exchange([blocks, stats], "gy", True, 1)
    stats = stats[:, :, :tok_rows].reshape(count_gy, 2, heads_here, tok_rows)
    stats = jnp.swapaxes(stats, 2, 3)
    factor = jnp.exp(stats[:, 0] - jnp.max(stats[:, 0], 0))
    denom = jnp.sum(stats[:, 1] * factor, 0)
    factor = factor / denom
    attn_part = jnp.sum(
        blocks.astype(jnp.float32).reshape(count_gy, tok_rows, heads_here, head_dim)
        * factor[..., None],
        0,
    )
    attn_part = attn_part.astype(jnp.bfloat16).reshape(tok_rows, heads_here * head_dim)
    (attn,) = exchange([attn_part], "gy", False, 2)
    attn = jnp.swapaxes(attn, 0, 1).reshape(tok_rows, q_cols)
    states_here = lax.dynamic_slice_in_dim(states, col_index * cols_here, cols_here, 1)
    resid = (
        states_here.astype(jnp.float32) + jnp.dot(attn, w_o, preferred_element_type=jnp.float32)
    ).astype(jnp.bfloat16)
    exp_here = w_in.shape[0]
    expert_count = exp_here * count_gx
    top_k = routing.shape[1]
    most_rows = 3 * tok_rows * top_k // (2 * expert_count)
    hidden_units = w_down.shape[1]
    gain_float = ffn_gain.astype(jnp.float32)
    tokens = routing.shape[0]
    slots = count_gx * most_rows
    own_experts = row_index * exp_here + jnp.arange(exp_here, dtype=jnp.int32)
    matched = routing[:, None, :] == own_experts[None, :, None]
    hits = jnp.any(matched, -1)
    weights = jnp.sum(jnp.where(matched, route_weight[:, None, :], 0.0), -1)
    order = jnp.arange(tok_rows, dtype=jnp.int32)
    earlier = (order[:, None] > order[None, :]).astype(jnp.bfloat16)
    rank = jnp.einsum(
        "tu,bue->bte",
        earlier,
        hits.astype(jnp.bfloat16).reshape(count_gx, tok_rows, exp_here),
        preferred_element_type=jnp.float32,
    ).astype(jnp.int32)
    first_slot = jnp.arange(count_gx, dtype=jnp.int32)[:, None, None] * most_rows
    slot_of = jnp.where(hits, (rank + first_slot).reshape(tokens, exp_here), -1)
    pick = slot_of.T[:, None, :] == jnp.arange(slots, dtype=jnp.int32)[None, :, None]
    pick_matrix = pick.astype(jnp.bfloat16)
    slot_weight = jnp.sum(jnp.where(pick, weights.T[:, None, :], 0.0), -1)
    (gathered,) = exchange([resid], "gx", False, 3)
    gathered = gathered.reshape(tokens, cols_here).astype(jnp.float32)
    token_squares = jnp.sum(gathered * gathered, -1)
    slot_squares = jnp.sum(jnp.where(pick, token_squares, 0.0), -1)
    piece = 16
    slot_squares = jnp.pad(slot_squares.reshape(-1, piece), ((0, 0), (0, 128 - piece)))
    scaled = (gathered * gain_float).astype(jnp.bfloat16)
    rows = jnp.einsum(
        "est,td->esd", pick_matrix, scaled, preferred_element_type=jnp.float32
    ).astype(jnp.bfloat16)
    hidden = expert_hidden(rows, slot_squares, w_in, model_width, 4)
    expert_out = jnp.einsum("esf,efd->esd", hidden, w_down, preferred_element_type=jnp.float32)
    expert_out = (expert_out * slot_weight[..., None]).astype(jnp.bfloat16)
    partial_moe = jnp.einsum(
        "est,esd->td", pick_matrix, expert_out, preferred_element_type=jnp.float32
    ).astype(jnp.bfloat16)
    (returned,) = exchange(
        [partial_moe.reshape(count_gx, tok_rows, cols_here)], "gx", True, 5
    )
    moe_total = jnp.sum(returned.astype(jnp.float32), 0)
    layer_out = (resid.astype(jnp.float32) + moe_total).astype(jnp.bfloat16)
    kv_new = jnp.concatenate([k_rot, qkv_whole[:, q_cols + kv_cols :]], -1)[None]
    accepted_kv = jnp.einsum(
        "rat,rtc->rac", accept.astype(jnp.bfloat16), kv_new, preferred_element_type=jnp.float32
    ).astype(jnp.bfloat16)
    return (layer_out, accepted_kv)


def solution(mesh):
    in_specs = (
        P("gx", None),
        P(),
        P(None, "gy"),
        P(),
        P(),
        P("gx", "gy", None),
        P("gx", "gy", None),
        P("gx"),
        P("gx", None, None),
        P(None, "gy"),
        P("gy"),
        P(),
        P(),
        P("gx", "gy", None),
        P("gx", None, "gy"),
        P("gx", None, None),
    )
    out_specs = (P("gx", "gy"), P("gx", None, None))
    return jax.shard_map(body, mesh=mesh, in_specs=in_specs, out_specs=out_specs, check_vma=False)
```

```python
import math

import jax
import jax.numpy as jnp
from jax import lax
from jax.experimental import pallas as pl
from jax.experimental.pallas import tpu as pltpu
from jax.sharding import PartitionSpec as P

EPS = 1e-06
NEG = -1e30
THETA_LOG = math.log(1000000.0)


MESH = pl.DeviceIdType.MESH


def exchange(arrays, axis, scatter, cid):
    count = lax.axis_size(axis)
    number = len(arrays)

    def kernel(*refs):
        ins, outs = refs[:number], refs[number : 2 * number]
        send, recv, local = refs[2 * number :]
        me = lax.axis_index(axis)
        barrier = pltpu.get_barrier_semaphore()
        for d in range(1, count):
            pl.semaphore_signal(
                barrier, inc=1, device_id={axis: lax.rem(me + d, count)}, device_id_type=MESH
            )
        pl.semaphore_wait(barrier, count - 1)
        copies = []
        for d in range(1, count):
            peer = lax.rem(me + d, count)
            for i in range(number):
                copy = pltpu.make_async_remote_copy(
                    src_ref=ins[i].at[peer] if scatter else ins[i],
                    dst_ref=outs[i].at[me],
                    send_sem=send.at[i, d],
                    recv_sem=recv.at[i, d],
                    device_id={axis: peer},
                    device_id_type=MESH,
                )
                copy.start()
                copies.append(copy)
        own = []
        for i in range(number):
            copy = pltpu.make_async_copy(
                ins[i].at[me] if scatter else ins[i], outs[i].at[me], local.at[i]
            )
            copy.start()
            own.append(copy)
        for copy in own + copies:
            copy.wait()

    outs = [
        jax.ShapeDtypeStruct(x.shape if scatter else (count,) + x.shape, x.dtype) for x in arrays
    ]
    return pl.pallas_call(
        kernel,
        out_shape=outs,
        in_specs=[pl.BlockSpec(memory_space=pltpu.VMEM)] * number,
        out_specs=[pl.BlockSpec(memory_space=pltpu.VMEM)] * number,
        scratch_shapes=[
            pltpu.SemaphoreType.DMA((number, count)),
            pltpu.SemaphoreType.DMA((number, count)),
            pltpu.SemaphoreType.DMA((number,)),
        ],
        compiler_params=pltpu.CompilerParams(collective_id=cid, has_side_effects=True),
        name="exchange_%d" % cid,
    )(*arrays)


def expert_hidden(rows, squares, w_in, model_width, cid):
    axis = "gy"
    count = lax.axis_size(axis)
    experts, slots, depth = rows.shape
    wide = w_in.shape[2]
    units = wide // 2
    half = experts // 2
    piece = 16
    sub = slots // piece
    chunks = half * sub
    hop = 2
    far = hop * (count - 1)

    def kernel(
        x_ref, sq_ref, w_hbm, hid_ref, wbuf, part, rbuf, sqbuf, inv_ref,
        wsem, rs_s, rs_r, h_s, h_r, sq_s, sq_r,
    ):
        me = lax.axis_index(axis)
        prev = lax.rem(me + count - 1, count)
        nxt = lax.rem(me + 1, count)
        at_low = me == 0
        at_high = me == count - 1

        def load(e):
            return pltpu.make_async_copy(w_hbm.at[e], wbuf.at[e], wsem.at[e])

        for s in range(half):
            load(half + s).start()
            load(s).start()
        barrier = pltpu.get_barrier_semaphore()
        for d in range(1, count):
            pl.semaphore_signal(
                barrier, inc=1, device_id={axis: lax.rem(me + d, count)}, device_id_type=MESH
            )
        pl.semaphore_wait(barrier, count - 1)

        def sq_copy(d):
            return pltpu.make_async_remote_copy(
                src_ref=sq_ref,
                dst_ref=sqbuf.at[d],
                send_sem=sq_s.at[d],
                recv_sem=sq_r.at[d],
                device_id={axis: lax.rem(me + d, count)},
                device_id_type=MESH,
            )

        for d in range(1, count):
            sq_copy(d).start()
        total = sq_ref[...]
        for d in range(1, count):
            sq_copy(d).wait()
            total = total + sqbuf[d]
        inv_ref[...] = lax.rsqrt(total / model_width + EPS)
        diagonal = lax.broadcasted_iota(jnp.int32, (piece, 128), 0) == lax.broadcasted_iota(
            jnp.int32, (piece, 128), 1
        )

        def rs_copy(h, c):
            return pltpu.make_async_remote_copy(
                src_ref=part.at[h, c],
                dst_ref=rbuf.at[h, c],
                send_sem=rs_s.at[h, c],
                recv_sem=rs_r.at[h, c],
                device_id={axis: nxt if h else prev},
                device_id_type=MESH,
            )

        def hid_copy(h, c):
            return pltpu.make_async_remote_copy(
                src_ref=hid_ref.at[h, c],
                dst_ref=hid_ref.at[h, c],
                send_sem=h_s.at[h, c],
                recv_sem=h_r.at[h, c],
                device_id={axis: prev if h else nxt},
                device_id_type=MESH,
            )

        def ends(h):
            return (at_low, at_high) if h else (at_high, at_low)

        def reduce_chunk(h, c):
            first, last = ends(h)

            @pl.when(jnp.logical_not(first))
            def _():
                rs_copy(h, c).wait_recv()

            @pl.when(jnp.logical_not(jnp.logical_or(first, last)))
            def _():
                part[h, c] = (
                    part[h, c].astype(jnp.float32) + rbuf[h, c].astype(jnp.float32)
                ).astype(jnp.bfloat16)

            @pl.when(jnp.logical_not(last))
            def _():
                rs_copy(h, c).start()

            @pl.when(last)
            def _():
                row = inv_ref[pl.ds(h * chunks + c, 1), :]
                inverse = jnp.sum(jnp.where(diagonal, row, 0.0), 1, keepdims=True)
                summed = part[h, c].astype(jnp.float32) + rbuf[h, c].astype(jnp.float32)
                gate = summed[:, :units] * inverse
                up = summed[:, units:] * inverse
                hid_ref[h, c] = (gate / (1.0 + jnp.exp(-gate)) * up).astype(jnp.bfloat16)
                hid_copy(h, c).start()

        def return_chunk(h, c):
            first, last = ends(h)

            @pl.when(jnp.logical_not(last))
            def _():
                hid_copy(h, c).wait_recv()

            @pl.when(jnp.logical_not(jnp.logical_or(first, last)))
            def _():
                hid_copy(h, c).start()

        def multiply(s):
            for h in (1, 0):
                e = h * half + s
                load(e).wait()
                value = jnp.dot(x_ref[e], wbuf[e], preferred_element_type=jnp.float32)
                for j in range(sub):
                    part[h, s * sub + j] = value[j * piece : (j + 1) * piece].astype(jnp.bfloat16)

        def step(t, carry):
            @pl.when(jnp.logical_and(t < chunks, lax.rem(t, sub) == 0))
            def _():
                multiply(lax.div(t, sub))

            for h in (1, 0):
                way = hop * (me if h else count - 1 - me)
                c = t - way

                @pl.when(jnp.logical_and(c >= 0, c < chunks))
                def _():
                    reduce_chunk(h, c)

            for h in (1, 0):
                way = hop * (me if h else count - 1 - me)
                b = t - 2 * far + way

                @pl.when(jnp.logical_and(b >= 0, b < chunks))
                def _():
                    return_chunk(h, b)

            return carry

        lax.fori_loop(0, chunks + 2 * far, step, 0)

        def finish(c, carry):
            for h in (1, 0):
                first, last = ends(h)

                @pl.when(jnp.logical_not(last))
                def _():
                    rs_copy(h, c).wait_send()

                @pl.when(jnp.logical_not(first))
                def _():
                    hid_copy(h, c).wait_send()

            return carry

        lax.fori_loop(0, chunks, finish, 0)

    hidden = pl.pallas_call(
        kernel,
        out_shape=jax.ShapeDtypeStruct((2, chunks, piece, units), jnp.bfloat16),
        in_specs=[
            pl.BlockSpec(memory_space=pltpu.VMEM),
            pl.BlockSpec(memory_space=pltpu.VMEM),
            pl.BlockSpec(memory_space=pl.ANY),
        ],
        out_specs=pl.BlockSpec(memory_space=pltpu.VMEM),
        scratch_shapes=[
            pltpu.VMEM((experts, depth, wide), jnp.bfloat16),
            pltpu.VMEM((2, chunks, piece, wide), jnp.bfloat16),
            pltpu.VMEM((2, chunks, piece, wide), jnp.bfloat16),
            pltpu.VMEM((count, 2 * chunks, 128), jnp.float32),
            pltpu.VMEM((2 * chunks, 128), jnp.float32),
            pltpu.SemaphoreType.DMA((experts,)),
            pltpu.SemaphoreType.DMA((2, chunks)),
            pltpu.SemaphoreType.DMA((2, chunks)),
            pltpu.SemaphoreType.DMA((2, chunks)),
            pltpu.SemaphoreType.DMA((2, chunks)),
            pltpu.SemaphoreType.DMA((count,)),
            pltpu.SemaphoreType.DMA((count,)),
        ],
        compiler_params=pltpu.CompilerParams(
            collective_id=cid, has_side_effects=True, vmem_limit_bytes=48 * 1024 * 1024
        ),
        name="expert_hidden",
    )(rows, squares, w_in)
    return hidden.reshape(experts, slots, units)


def attention_block(
    qkv, q_gain, k_gain, cosine, sine, cache_k, cache_v, limit, tree_mask, states_here, w_o, cid
):
    blocks = lax.axis_size("gy")
    rows_gx = lax.axis_size("gx")
    tokens = qkv.shape[0]
    span, kv_cols = cache_k.shape
    dim = q_gain.shape[1]
    kv_heads = kv_cols // dim
    heads = qkv.shape[1] // dim - 2 * kv_heads
    group = heads // kv_heads
    per_block = heads // blocks
    blocks_here = blocks // kv_heads
    width = per_block * dim
    cols = w_o.shape[1]
    scale = dim ** (-0.5)

    def kernel(
        limit_ref, q_ref, qg_ref, kg_ref, cos_ref, sin_ref, k_ref, v_ref, mask_ref, st_ref, wo_hbm,
        h_ref, rot_ref,
        acc_out, stat_out, acc_in, stat_in, attn, wo,
        wo_sem, a_s, a_r, s_s, s_r, t_s, t_r, h_s, h_r,
    ):
        me = lax.axis_index("gy")
        row = lax.axis_index("gx")
        load = pltpu.make_async_copy(wo_hbm, wo, wo_sem)
        load.start()
        barrier = pltpu.get_barrier_semaphore()
        for axis, here, count in (("gy", me, blocks), ("gx", row, rows_gx)):
            for d in range(1, count):
                pl.semaphore_signal(
                    barrier, inc=1, device_id={axis: lax.rem(here + d, count)}, device_id_type=MESH
                )
        pl.semaphore_wait(barrier, blocks + rows_gx - 2)

        def send(src, dst, send_sem, recv_sem, axis, peer):
            return pltpu.make_async_remote_copy(
                src_ref=src,
                dst_ref=dst,
                send_sem=send_sem,
                recv_sem=recv_sem,
                device_id={axis: peer},
                device_id_type=MESH,
            )

        def part_copies(block, source):
            return (
                send(acc_out.at[block], acc_in.at[source], a_s.at[block], a_r.at[source], "gy", block),
                send(stat_out.at[block], stat_in.at[source], s_s.at[block], s_r.at[source], "gy", block),
            )

        cos = cos_ref[...]
        sin = sin_ref[...]

        def turn(value, gain):
            value = value.astype(jnp.float32)
            value = value * lax.rsqrt(jnp.mean(value * value, -1, keepdims=True) + EPS) * gain
            return (value * cos + pltpu.roll(value, dim // 2, 1) * sin).astype(jnp.bfloat16)

        q_gain_row = qg_ref[...].astype(jnp.float32)
        k_gain_row = kg_ref[...].astype(jnp.float32)
        contract = (((1,), (1,)), ((), ()))
        diagonal = lax.broadcasted_iota(jnp.int32, (tokens, 128), 0) == lax.broadcasted_iota(
            jnp.int32, (tokens, 128), 1
        )

        def one_head(i, carry):
            g = lax.rem(lax.div(me, blocks_here) + 1 + i, kv_heads)

            def lanes(first, size):
                return pl.ds(pl.multiple_of(first, 128), size)

            query = jnp.concatenate(
                [
                    turn(q_ref[:, lanes((g * group + j) * dim, dim)], q_gain_row)
                    for j in range(group)
                ],
                0,
            )
            keys = turn(q_ref[:, lanes((heads + g) * dim, dim)], k_gain_row)
            values = q_ref[:, lanes((heads + kv_heads + g) * dim, dim)]
            rot_ref[:, lanes(g * dim, dim)] = keys
            tree = (
                lax.dot_general(query, keys, contract, preferred_element_type=jnp.float32) * scale
            )
            mask = jnp.concatenate([mask_ref[...]] * group, 0)
            tree_ok = jnp.logical_and(mask == 1, me == 0)
            tree = jnp.where(tree_ok, tree, NEG)
            score = (
                lax.dot_general(
                    query,
                    k_ref[:, lanes(g * dim, dim)],
                    contract,
                    preferred_element_type=jnp.float32,
                )
                * scale
            )
            valid = lax.broadcasted_iota(jnp.int32, score.shape, 1) < limit_ref[0]
            score = jnp.where(valid, score, NEG)
            top = jnp.maximum(jnp.max(score, 1, keepdims=True), jnp.max(tree, 1, keepdims=True))
            prob = jnp.where(valid, jnp.exp(score - top), 0.0).astype(jnp.bfloat16)
            prob_tree = jnp.where(tree_ok, jnp.exp(tree - top), 0.0).astype(jnp.bfloat16)
            total = jnp.sum(prob.astype(jnp.float32), 1, keepdims=True) + jnp.sum(
                prob_tree.astype(jnp.float32), 1, keepdims=True
            )
            acc = jnp.dot(prob, v_ref[:, lanes(g * dim, dim)], preferred_element_type=jnp.float32)
            acc = acc + jnp.dot(prob_tree, values, preferred_element_type=jnp.float32)
            acc = acc.astype(jnp.bfloat16)
            for b in range(blocks_here):
                block = g * blocks_here + b
                for place in range(per_block):
                    j = b * per_block + place
                    rows = slice(j * tokens, (j + 1) * tokens)
                    acc_out[block, :, place * dim : (place + 1) * dim] = acc[rows]
                    for k, column in enumerate((top, total)):
                        stat_out[block, k * per_block + place : k * per_block + place + 1, :] = (
                            jnp.sum(jnp.where(diagonal, column[rows], 0.0), 0, keepdims=True)
                        )

                @pl.when(block != me)
                def _():
                    for copy in part_copies(block, me):
                        copy.start()

            return carry

        lax.fori_loop(0, kv_heads, one_head, 0)

        acc_in[me] = acc_out[me]
        stat_in[me] = stat_out[me]
        for d in range(1, blocks):
            source = lax.rem(me + d, blocks)
            for copy in part_copies(source, source):
                copy.wait_recv()
        tops = [stat_in[j, :per_block, :] for j in range(blocks)]
        best = tops[0]
        for j in range(1, blocks):
            best = jnp.maximum(best, tops[j])
        factors = [jnp.exp(tops[j] - best) for j in range(blocks)]
        denom = stat_in[0, per_block:, :] * factors[0]
        for j in range(1, blocks):
            denom = denom + stat_in[j, per_block:, :] * factors[j]
        for place in range(per_block):
            joined = jnp.zeros((tokens, dim), jnp.float32)
            for j in range(blocks):
                line = (factors[j] / denom)[place : place + 1, :]
                column = jnp.sum(jnp.where(diagonal, line, 0.0), 1, keepdims=True)
                joined = joined + column * acc_in[
                    j, :, place * dim : (place + 1) * dim
                ].astype(jnp.float32)
            attn[me, :, place * dim : (place + 1) * dim] = joined.astype(jnp.bfloat16)

        def attn_copy(d, source):
            return send(
                attn.at[source], attn.at[source], t_s.at[d], t_r.at[d], "gy", lax.rem(me + d, blocks)
            )

        for d in range(1, blocks):
            attn_copy(d, me).start()
        load.wait()

        def project(source):
            return jnp.dot(
                attn[source],
                wo[pl.ds(pl.multiple_of(source * width, width), width), :],
                preferred_element_type=jnp.float32,
            )

        total = st_ref[...].astype(jnp.float32) + project(me)
        for d in range(1, blocks):
            source = lax.rem(me + blocks - d, blocks)
            attn_copy(d, source).wait_recv()
            total = total + project(source)
        h_ref[row] = total.astype(jnp.bfloat16)

        def h_copy(d, source):
            return send(
                h_ref.at[source], h_ref.at[source], h_s.at[d], h_r.at[d], "gx",
                lax.rem(row + d, rows_gx),
            )

        for d in range(1, rows_gx):
            h_copy(d, row).start()
        for d in range(1, blocks):
            block = lax.rem(me + d, blocks)
            for copy in part_copies(block, me):
                copy.wait_send()
            attn_copy(d, me).wait_send()
        for d in range(1, rows_gx):
            h_copy(d, lax.rem(row + rows_gx - d, rows_gx)).wait_recv()
            h_copy(d, row).wait_send()

    vmem = pl.BlockSpec(memory_space=pltpu.VMEM)
    dma = pltpu.SemaphoreType.DMA
    return pl.pallas_call(
        kernel,
        out_shape=[
            jax.ShapeDtypeStruct((rows_gx, tokens, cols), jnp.bfloat16),
            jax.ShapeDtypeStruct((tokens, kv_cols), jnp.bfloat16),
        ],
        in_specs=[pl.BlockSpec(memory_space=pltpu.SMEM)]
        + [vmem] * 9
        + [pl.BlockSpec(memory_space=pl.ANY)],
        out_specs=[vmem, vmem],
        scratch_shapes=[
            pltpu.VMEM((blocks, tokens, width), jnp.bfloat16),
            pltpu.VMEM((blocks, 2 * per_block, 128), jnp.float32),
            pltpu.VMEM((blocks, tokens, width), jnp.bfloat16),
            pltpu.VMEM((blocks, 2 * per_block, 128), jnp.float32),
            pltpu.VMEM((blocks, tokens, width), jnp.bfloat16),
            pltpu.VMEM(w_o.shape, jnp.bfloat16),
            dma,
            dma((blocks,)),
            dma((blocks,)),
            dma((blocks,)),
            dma((blocks,)),
            dma((blocks,)),
            dma((blocks,)),
            dma((rows_gx,)),
            dma((rows_gx,)),
        ],
        compiler_params=pltpu.CompilerParams(
            collective_id=cid, has_side_effects=True, vmem_limit_bytes=48 * 1024 * 1024
        ),
        name="attention_block",
    )(
        limit, qkv, q_gain, k_gain, cosine, sine, cache_k, cache_v, tree_mask, states_here, w_o
    )


def rms_scale(values, gain):
    return values * lax.rsqrt(jnp.mean(values * values, -1, keepdims=True) + EPS) * gain


def angles_of(position, dim):
    freqs = jnp.exp(jnp.arange(dim // 2, dtype=jnp.float32) * (-2.0 * THETA_LOG / dim))
    angles = position.astype(jnp.float32)[..., None] * freqs
    cosine = jnp.cos(angles)
    sine = jnp.sin(angles)
    return jnp.concatenate([cosine, cosine], -1), jnp.concatenate([-sine, sine], -1)


def body(
    states,
    attn_gain,
    w_qkv,
    q_gain,
    k_gain,
    cache_k,
    cache_v,
    cache_len,
    tree_mask,
    w_o,
    ffn_gain,
    routing,
    route_weight,
    w_in,
    w_down,
    accept,
):
    tok_rows, model_width = states.shape
    head_dim = q_gain.shape[0]
    kv_cols = cache_k.shape[2]
    heads_all = w_o.shape[0] // head_dim
    cache_span = cache_k.shape[1]
    cols_here = w_o.shape[1]
    col_index = lax.axis_index("gy")
    row_index = lax.axis_index("gx")
    count_gx = lax.axis_size("gx")
    normed = rms_scale(states.astype(jnp.float32), attn_gain.astype(jnp.float32)).astype(
        jnp.bfloat16
    )
    qkv_part = jnp.dot(normed, w_qkv, preferred_element_type=jnp.float32).astype(jnp.bfloat16)
    (qkv_blocks,) = exchange([qkv_part], "gy", False, 0)
    qkv_whole = jnp.swapaxes(qkv_blocks, 0, 1).reshape(tok_rows, -1)
    q_cols = heads_all * head_dim
    depth = jnp.sum(tree_mask, -1) - 1
    cosine, sine = angles_of((cache_len[:, None] + depth)[0], head_dim)
    states_here = lax.dynamic_slice_in_dim(states, col_index * cols_here, cols_here, 1)
    gathered, k_rot = attention_block(
        qkv_whole,
        q_gain[None],
        k_gain[None],
        cosine,
        sine,
        cache_k[0],
        cache_v[0],
        cache_len - col_index * cache_span,
        tree_mask[0],
        states_here,
        w_o,
        1,
    )
    resid = lax.dynamic_index_in_dim(gathered, row_index, 0, False)
    exp_here = w_in.shape[0]
    expert_count = exp_here * count_gx
    top_k = routing.shape[1]
    most_rows = 3 * tok_rows * top_k // (2 * expert_count)
    hidden_units = w_down.shape[1]
    gain_float = ffn_gain.astype(jnp.float32)
    tokens = routing.shape[0]
    slots = count_gx * most_rows
    own_experts = row_index * exp_here + jnp.arange(exp_here, dtype=jnp.int32)
    matched = routing[:, None, :] == own_experts[None, :, None]
    hits = jnp.any(matched, -1)
    weights = jnp.sum(jnp.where(matched, route_weight[:, None, :], 0.0), -1)
    order = jnp.arange(tok_rows, dtype=jnp.int32)
    earlier = (order[:, None] > order[None, :]).astype(jnp.bfloat16)
    rank = jnp.einsum(
        "tu,bue->bte",
        earlier,
        hits.astype(jnp.bfloat16).reshape(count_gx, tok_rows, exp_here),
        preferred_element_type=jnp.float32,
    ).astype(jnp.int32)
    first_slot = jnp.arange(count_gx, dtype=jnp.int32)[:, None, None] * most_rows
    slot_of = jnp.where(hits, (rank + first_slot).reshape(tokens, exp_here), -1)
    pick = slot_of.T[:, None, :] == jnp.arange(slots, dtype=jnp.int32)[None, :, None]
    pick_matrix = pick.astype(jnp.bfloat16)
    slot_weight = jnp.sum(jnp.where(pick, weights.T[:, None, :], 0.0), -1)
    gathered = gathered.reshape(tokens, cols_here).astype(jnp.float32)
    token_squares = jnp.sum(gathered * gathered, -1)
    slot_squares = jnp.sum(jnp.where(pick, token_squares, 0.0), -1)
    piece = 16
    slot_squares = jnp.pad(slot_squares.reshape(-1, piece), ((0, 0), (0, 128 - piece)))
    scaled = (gathered * gain_float).astype(jnp.bfloat16)
    rows = jnp.einsum(
        "est,td->esd", pick_matrix, scaled, preferred_element_type=jnp.float32
    ).astype(jnp.bfloat16)
    hidden = expert_hidden(rows, slot_squares, w_in, model_width, 4)
    expert_out = jnp.einsum("esf,efd->esd", hidden, w_down, preferred_element_type=jnp.float32)
    expert_out = (expert_out * slot_weight[..., None]).astype(jnp.bfloat16)
    partial_moe = jnp.einsum(
        "est,esd->td", pick_matrix, expert_out, preferred_element_type=jnp.float32
    ).astype(jnp.bfloat16)
    (returned,) = exchange(
        [partial_moe.reshape(count_gx, tok_rows, cols_here)], "gx", True, 5
    )
    moe_total = jnp.sum(returned.astype(jnp.float32), 0)
    layer_out = (resid.astype(jnp.float32) + moe_total).astype(jnp.bfloat16)
    kv_new = jnp.concatenate([k_rot, qkv_whole[:, q_cols + kv_cols :]], -1)[None]
    accepted_kv = jnp.einsum(
        "rat,rtc->rac", accept.astype(jnp.bfloat16), kv_new, preferred_element_type=jnp.float32
    ).astype(jnp.bfloat16)
    return (layer_out, accepted_kv)


def solution(mesh):
    in_specs = (
        P("gx", None),
        P(),
        P(None, "gy"),
        P(),
        P(),
        P("gx", "gy", None),
        P("gx", "gy", None),
        P("gx"),
        P("gx", None, None),
        P(None, "gy"),
        P("gy"),
        P(),
        P(),
        P("gx", "gy", None),
        P("gx", None, "gy"),
        P("gx", None, None),
    )
    out_specs = (P("gx", "gy"), P("gx", None, None))
    return jax.shard_map(body, mesh=mesh, in_specs=in_specs, out_specs=out_specs, check_vma=False)
```

```python
import math

import jax
import jax.numpy as jnp
from jax import lax
from jax.experimental import pallas as pl
from jax.experimental.pallas import tpu as pltpu
from jax.sharding import PartitionSpec as P

EPS = 1e-06
NEG = -1e30
THETA_LOG = math.log(1000000.0)


MESH = pl.DeviceIdType.MESH


def exchange(arrays, axis, scatter, cid):
    count = lax.axis_size(axis)
    number = len(arrays)

    def kernel(*refs):
        ins, outs = refs[:number], refs[number : 2 * number]
        send, recv, local = refs[2 * number :]
        me = lax.axis_index(axis)
        barrier = pltpu.get_barrier_semaphore()
        for d in range(1, count):
            pl.semaphore_signal(
                barrier, inc=1, device_id={axis: lax.rem(me + d, count)}, device_id_type=MESH
            )
        pl.semaphore_wait(barrier, count - 1)
        copies = []
        for d in range(1, count):
            peer = lax.rem(me + d, count)
            for i in range(number):
                copy = pltpu.make_async_remote_copy(
                    src_ref=ins[i].at[peer] if scatter else ins[i],
                    dst_ref=outs[i].at[me],
                    send_sem=send.at[i, d],
                    recv_sem=recv.at[i, d],
                    device_id={axis: peer},
                    device_id_type=MESH,
                )
                copy.start()
                copies.append(copy)
        own = []
        for i in range(number):
            copy = pltpu.make_async_copy(
                ins[i].at[me] if scatter else ins[i], outs[i].at[me], local.at[i]
            )
            copy.start()
            own.append(copy)
        for copy in own + copies:
            copy.wait()

    outs = [
        jax.ShapeDtypeStruct(x.shape if scatter else (count,) + x.shape, x.dtype) for x in arrays
    ]
    return pl.pallas_call(
        kernel,
        out_shape=outs,
        in_specs=[pl.BlockSpec(memory_space=pltpu.VMEM)] * number,
        out_specs=[pl.BlockSpec(memory_space=pltpu.VMEM)] * number,
        scratch_shapes=[
            pltpu.SemaphoreType.DMA((number, count)),
            pltpu.SemaphoreType.DMA((number, count)),
            pltpu.SemaphoreType.DMA((number,)),
        ],
        compiler_params=pltpu.CompilerParams(collective_id=cid, has_side_effects=True),
        name="exchange_%d" % cid,
    )(*arrays)


def expert_layer(rows, squares, w_in, w_down, slot_weight, pick_back, resid, model_width, cid):
    axis = "gy"
    count = lax.axis_size(axis)
    peers = lax.axis_size("gx")
    experts, slots, depth = rows.shape
    tokens, cols = resid.shape
    wide = w_in.shape[2]
    units = wide // 2
    half = experts // 2
    piece = 16
    sub = slots // piece
    chunks = half * sub
    hop = 2
    far = hop * (count - 1)

    def kernel(
        x_ref, sq_ref, weight_ref, pick_ref, resid_ref, w_hbm, d_hbm, out_ref,
        hid_ref, wbuf, dbuf, part, rbuf, sqbuf, inv_ref, obuf, pbuf, ret,
        wsem, dsem, rs_s, rs_r, h_s, h_r, sq_s, sq_r, g_s, g_r,
    ):
        me = lax.axis_index(axis)
        prev = lax.rem(me + count - 1, count)
        nxt = lax.rem(me + 1, count)
        at_low = me == 0
        at_high = me == count - 1

        def load(e):
            return pltpu.make_async_copy(w_hbm.at[e], wbuf.at[e], wsem.at[e])

        def load_down(e):
            return pltpu.make_async_copy(d_hbm.at[e], dbuf.at[e], dsem.at[e])

        row = lax.axis_index("gx")
        for s in range(half):
            load(half + s).start()
            load(s).start()
        for s in range(half):
            load_down(half + s).start()
            load_down(s).start()
        barrier = pltpu.get_barrier_semaphore()
        for d in range(1, count):
            pl.semaphore_signal(
                barrier, inc=1, device_id={axis: lax.rem(me + d, count)}, device_id_type=MESH
            )
        for d in range(1, peers):
            pl.semaphore_signal(
                barrier, inc=1, device_id={"gx": lax.rem(row + d, peers)}, device_id_type=MESH
            )

        def multiply(h, s):
            e = h * half + s
            load(e).wait()
            value = jnp.dot(x_ref[e], wbuf[e], preferred_element_type=jnp.float32)
            for j in range(sub):
                part[h, s * sub + j] = value[j * piece : (j + 1) * piece].astype(jnp.bfloat16)

        multiply(1, 0)
        multiply(0, 0)
        pl.semaphore_wait(barrier, count + peers - 2)

        def sq_copy(d):
            return pltpu.make_async_remote_copy(
                src_ref=sq_ref,
                dst_ref=sqbuf.at[d],
                send_sem=sq_s.at[d],
                recv_sem=sq_r.at[d],
                device_id={axis: lax.rem(me + d, count)},
                device_id_type=MESH,
            )

        for d in range(1, count):
            sq_copy(d).start()

        def finish_squares():
            total = sq_ref[...]
            for d in range(1, count):
                sq_copy(d).wait()
                total = total + sqbuf[d]
            inv_ref[...] = lax.rsqrt(total / model_width + EPS)

        diagonal = lax.broadcasted_iota(jnp.int32, (piece, 128), 0) == lax.broadcasted_iota(
            jnp.int32, (piece, 128), 1
        )

        def rs_copy(h, c):
            return pltpu.make_async_remote_copy(
                src_ref=part.at[h, c],
                dst_ref=rbuf.at[h, c],
                send_sem=rs_s.at[h, c],
                recv_sem=rs_r.at[h, c],
                device_id={axis: nxt if h else prev},
                device_id_type=MESH,
            )

        def hid_copy(h, c):
            return pltpu.make_async_remote_copy(
                src_ref=hid_ref.at[h, c],
                dst_ref=hid_ref.at[h, c],
                send_sem=h_s.at[h, c],
                recv_sem=h_r.at[h, c],
                device_id={axis: prev if h else nxt},
                device_id_type=MESH,
            )

        def ends(h):
            return (at_low, at_high) if h else (at_high, at_low)

        def reduce_chunk(h, c):
            first, last = ends(h)

            @pl.when(jnp.logical_not(first))
            def _():
                rs_copy(h, c).wait_recv()

            @pl.when(jnp.logical_not(jnp.logical_or(first, last)))
            def _():
                part[h, c] = (
                    part[h, c].astype(jnp.float32) + rbuf[h, c].astype(jnp.float32)
                ).astype(jnp.bfloat16)

            @pl.when(jnp.logical_not(last))
            def _():
                rs_copy(h, c).start()

            @pl.when(last)
            def _():
                row = inv_ref[pl.ds(h * chunks + c, 1), :]
                inverse = jnp.sum(jnp.where(diagonal, row, 0.0), 1, keepdims=True)
                summed = part[h, c].astype(jnp.float32) + rbuf[h, c].astype(jnp.float32)
                gate = summed[:, :units] * inverse
                up = summed[:, units:] * inverse
                hid_ref[h, c] = (gate / (1.0 + jnp.exp(-gate)) * up).astype(jnp.bfloat16)
                hid_copy(h, c).start()

        def return_chunk(h, c):
            first, last = ends(h)

            @pl.when(jnp.logical_not(last))
            def _():
                hid_copy(h, c).wait_recv()

            @pl.when(jnp.logical_not(jnp.logical_or(first, last)))
            def _():
                hid_copy(h, c).start()

        def project(h, s):
            e = h * half + s
            load_down(e).wait()
            value = hid_ref[h, pl.ds(s * sub, sub)].reshape(slots, units)
            value = jnp.dot(value, dbuf[e], preferred_element_type=jnp.float32)
            obuf[e] = (value * weight_ref[e]).astype(jnp.bfloat16)

        def step(t, carry):
            for h, place in ((1, 1), (0, sub // 2 + 1)):

                @pl.when(jnp.logical_and(t < chunks - sub, lax.rem(t, sub) == place))
                def _():
                    multiply(h, lax.div(t, sub) + 1)

            @pl.when(t == far - 1)
            def _():
                finish_squares()

            for h in (1, 0):
                way = hop * (me if h else count - 1 - me)
                c = t - way

                @pl.when(jnp.logical_and(c >= 0, c < chunks))
                def _():
                    reduce_chunk(h, c)

            for h in (1, 0):
                way = hop * (me if h else count - 1 - me)
                b = t - 2 * far + way

                @pl.when(jnp.logical_and(b >= 0, b < chunks))
                def _():
                    return_chunk(h, b)

                    @pl.when(lax.rem(b, sub) == sub - 1)
                    def _():
                        project(h, lax.div(b, sub))

            return carry

        lax.fori_loop(0, chunks + 2 * far, step, 0)

        def finish(c, carry):
            for h in (1, 0):
                first, last = ends(h)

                @pl.when(jnp.logical_not(last))
                def _():
                    rs_copy(h, c).wait_send()

                @pl.when(jnp.logical_not(first))
                def _():
                    hid_copy(h, c).wait_send()

            return carry

        summed = jnp.dot(
            pick_ref[...],
            obuf[...].reshape(experts * slots, cols),
            preferred_element_type=jnp.float32,
        )
        for p in range(peers):
            pbuf[p] = summed[p * tokens : (p + 1) * tokens].astype(jnp.bfloat16)

        def back_copy(d):
            peer = lax.rem(row + d, peers)
            return pltpu.make_async_remote_copy(
                src_ref=pbuf.at[peer],
                dst_ref=ret.at[d],
                send_sem=g_s.at[d],
                recv_sem=g_r.at[d],
                device_id={"gx": peer},
                device_id_type=MESH,
            )

        for d in range(1, peers):
            back_copy(d).start()
        moe = pbuf[row].astype(jnp.float32)
        lax.fori_loop(0, chunks, finish, 0)
        for d in range(1, peers):
            back_copy(d).wait_recv()
            moe = moe + ret[d].astype(jnp.float32)
        out_ref[...] = (resid_ref[...].astype(jnp.float32) + moe).astype(jnp.bfloat16)
        for d in range(1, peers):
            back_copy(d).wait_send()

    vmem = pl.BlockSpec(memory_space=pltpu.VMEM)
    hbm = pl.BlockSpec(memory_space=pl.ANY)
    dma = pltpu.SemaphoreType.DMA
    return pl.pallas_call(
        kernel,
        out_shape=jax.ShapeDtypeStruct((tokens, cols), jnp.bfloat16),
        in_specs=[vmem] * 5 + [hbm, hbm],
        out_specs=vmem,
        scratch_shapes=[
            pltpu.VMEM((2, chunks, piece, units), jnp.bfloat16),
            pltpu.VMEM((experts, depth, wide), jnp.bfloat16),
            pltpu.VMEM((experts, units, cols), jnp.bfloat16),
            pltpu.VMEM((2, chunks, piece, wide), jnp.bfloat16),
            pltpu.VMEM((2, chunks, piece, wide), jnp.bfloat16),
            pltpu.VMEM((count, 2 * chunks, 128), jnp.float32),
            pltpu.VMEM((2 * chunks, 128), jnp.float32),
            pltpu.VMEM((experts, slots, cols), jnp.bfloat16),
            pltpu.VMEM((peers, tokens, cols), jnp.bfloat16),
            pltpu.VMEM((peers, tokens, cols), jnp.bfloat16),
            dma((experts,)),
            dma((experts,)),
            dma((2, chunks)),
            dma((2, chunks)),
            dma((2, chunks)),
            dma((2, chunks)),
            dma((count,)),
            dma((count,)),
            dma((peers,)),
            dma((peers,)),
        ],
        compiler_params=pltpu.CompilerParams(
            collective_id=cid, has_side_effects=True, vmem_limit_bytes=52 * 1024 * 1024
        ),
        name="expert_layer",
    )(rows, squares, slot_weight, pick_back, resid, w_in, w_down)


def attention_block(
    qkv, q_gain, k_gain, cosine, sine, cache_k, cache_v, limit, tree_mask, states_here, w_o, cid
):
    blocks = lax.axis_size("gy")
    rows_gx = lax.axis_size("gx")
    tokens = qkv.shape[0]
    span, kv_cols = cache_k.shape
    dim = q_gain.shape[1]
    kv_heads = kv_cols // dim
    heads = qkv.shape[1] // dim - 2 * kv_heads
    group = heads // kv_heads
    per_block = heads // blocks
    blocks_here = blocks // kv_heads
    width = per_block * dim
    cols = w_o.shape[1]
    scale = dim ** (-0.5)

    def kernel(
        limit_ref, q_ref, qg_ref, kg_ref, cos_ref, sin_ref, k_ref, v_ref, mask_ref, st_ref, wo_hbm,
        h_ref, rot_ref,
        acc_out, stat_out, acc_in, stat_in, attn, wo,
        wo_sem, a_s, a_r, s_s, s_r, t_s, t_r, h_s, h_r,
    ):
        me = lax.axis_index("gy")
        row = lax.axis_index("gx")
        load = pltpu.make_async_copy(wo_hbm, wo, wo_sem)
        load.start()
        barrier = pltpu.get_barrier_semaphore()
        for axis, here, count in (("gy", me, blocks), ("gx", row, rows_gx)):
            for d in range(1, count):
                pl.semaphore_signal(
                    barrier, inc=1, device_id={axis: lax.rem(here + d, count)}, device_id_type=MESH
                )
        pl.semaphore_wait(barrier, blocks + rows_gx - 2)

        def send(src, dst, send_sem, recv_sem, axis, peer):
            return pltpu.make_async_remote_copy(
                src_ref=src,
                dst_ref=dst,
                send_sem=send_sem,
                recv_sem=recv_sem,
                device_id={axis: peer},
                device_id_type=MESH,
            )

        def part_copies(block, source):
            return (
                send(acc_out.at[block], acc_in.at[source], a_s.at[block], a_r.at[source], "gy", block),
                send(stat_out.at[block], stat_in.at[source], s_s.at[block], s_r.at[source], "gy", block),
            )

        cos = cos_ref[...]
        sin = sin_ref[...]

        def turn(value, gain):
            value = value.astype(jnp.float32)
            value = value * lax.rsqrt(jnp.mean(value * value, -1, keepdims=True) + EPS) * gain
            return (value * cos + pltpu.roll(value, dim // 2, 1) * sin).astype(jnp.bfloat16)

        q_gain_row = qg_ref[...].astype(jnp.float32)
        k_gain_row = kg_ref[...].astype(jnp.float32)
        contract = (((1,), (1,)), ((), ()))
        diagonal = lax.broadcasted_iota(jnp.int32, (tokens, 128), 0) == lax.broadcasted_iota(
            jnp.int32, (tokens, 128), 1
        )

        def one_head(i, carry):
            g = lax.rem(lax.div(me, blocks_here) + 1 + i, kv_heads)

            def lanes(first, size):
                return pl.ds(pl.multiple_of(first, 128), size)

            query = jnp.concatenate(
                [
                    turn(q_ref[:, lanes((g * group + j) * dim, dim)], q_gain_row)
                    for j in range(group)
                ],
                0,
            )
            keys = turn(q_ref[:, lanes((heads + g) * dim, dim)], k_gain_row)
            values = q_ref[:, lanes((heads + kv_heads + g) * dim, dim)]
            rot_ref[:, lanes(g * dim, dim)] = keys
            tree = (
                lax.dot_general(query, keys, contract, preferred_element_type=jnp.float32) * scale
            )
            mask = jnp.concatenate([mask_ref[...]] * group, 0)
            tree_ok = jnp.logical_and(mask == 1, me == 0)
            tree = jnp.where(tree_ok, tree, NEG)
            score = (
                lax.dot_general(
                    query,
                    k_ref[:, lanes(g * dim, dim)],
                    contract,
                    preferred_element_type=jnp.float32,
                )
                * scale
            )
            valid = lax.broadcasted_iota(jnp.int32, score.shape, 1) < limit_ref[0]
            score = jnp.where(valid, score, NEG)
            top = jnp.maximum(jnp.max(score, 1, keepdims=True), jnp.max(tree, 1, keepdims=True))
            prob = jnp.where(valid, jnp.exp(score - top), 0.0).astype(jnp.bfloat16)
            prob_tree = jnp.where(tree_ok, jnp.exp(tree - top), 0.0).astype(jnp.bfloat16)
            total = jnp.sum(prob.astype(jnp.float32), 1, keepdims=True) + jnp.sum(
                prob_tree.astype(jnp.float32), 1, keepdims=True
            )
            acc = jnp.dot(prob, v_ref[:, lanes(g * dim, dim)], preferred_element_type=jnp.float32)
            acc = acc + jnp.dot(prob_tree, values, preferred_element_type=jnp.float32)
            acc = acc.astype(jnp.bfloat16)
            for b in range(blocks_here):
                block = g * blocks_here + b
                for place in range(per_block):
                    j = b * per_block + place
                    rows = slice(j * tokens, (j + 1) * tokens)
                    acc_out[block, :, place * dim : (place + 1) * dim] = acc[rows]
                    for k, column in enumerate((top, total)):
                        stat_out[block, k * per_block + place : k * per_block + place + 1, :] = (
                            jnp.sum(jnp.where(diagonal, column[rows], 0.0), 0, keepdims=True)
                        )

                @pl.when(block != me)
                def _():
                    for copy in part_copies(block, me):
                        copy.start()

            return carry

        lax.fori_loop(0, kv_heads, one_head, 0)

        acc_in[me] = acc_out[me]
        stat_in[me] = stat_out[me]
        for d in range(1, blocks):
            source = lax.rem(me + d, blocks)
            for copy in part_copies(source, source):
                copy.wait_recv()
        tops = [stat_in[j, :per_block, :] for j in range(blocks)]
        best = tops[0]
        for j in range(1, blocks):
            best = jnp.maximum(best, tops[j])
        factors = [jnp.exp(tops[j] - best) for j in range(blocks)]
        denom = stat_in[0, per_block:, :] * factors[0]
        for j in range(1, blocks):
            denom = denom + stat_in[j, per_block:, :] * factors[j]
        for place in range(per_block):
            joined = jnp.zeros((tokens, dim), jnp.float32)
            for j in range(blocks):
                line = (factors[j] / denom)[place : place + 1, :]
                column = jnp.sum(jnp.where(diagonal, line, 0.0), 1, keepdims=True)
                joined = joined + column * acc_in[
                    j, :, place * dim : (place + 1) * dim
                ].astype(jnp.float32)
            attn[me, :, place * dim : (place + 1) * dim] = joined.astype(jnp.bfloat16)

        def attn_copy(d, source):
            return send(
                attn.at[source], attn.at[source], t_s.at[d], t_r.at[d], "gy", lax.rem(me + d, blocks)
            )

        for d in range(1, blocks):
            attn_copy(d, me).start()
        load.wait()

        def project(source):
            return jnp.dot(
                attn[source],
                wo[pl.ds(pl.multiple_of(source * width, width), width), :],
                preferred_element_type=jnp.float32,
            )

        total = st_ref[...].astype(jnp.float32) + project(me)
        for d in range(1, blocks):
            source = lax.rem(me + blocks - d, blocks)
            attn_copy(d, source).wait_recv()
            total = total + project(source)
        h_ref[row] = total.astype(jnp.bfloat16)

        def h_copy(d, source):
            return send(
                h_ref.at[source], h_ref.at[source], h_s.at[d], h_r.at[d], "gx",
                lax.rem(row + d, rows_gx),
            )

        for d in range(1, rows_gx):
            h_copy(d, row).start()
        for d in range(1, blocks):
            block = lax.rem(me + d, blocks)
            for copy in part_copies(block, me):
                copy.wait_send()
            attn_copy(d, me).wait_send()
        for d in range(1, rows_gx):
            h_copy(d, lax.rem(row + rows_gx - d, rows_gx)).wait_recv()
            h_copy(d, row).wait_send()

    vmem = pl.BlockSpec(memory_space=pltpu.VMEM)
    dma = pltpu.SemaphoreType.DMA
    return pl.pallas_call(
        kernel,
        out_shape=[
            jax.ShapeDtypeStruct((rows_gx, tokens, cols), jnp.bfloat16),
            jax.ShapeDtypeStruct((tokens, kv_cols), jnp.bfloat16),
        ],
        in_specs=[pl.BlockSpec(memory_space=pltpu.SMEM)]
        + [vmem] * 9
        + [pl.BlockSpec(memory_space=pl.ANY)],
        out_specs=[vmem, vmem],
        scratch_shapes=[
            pltpu.VMEM((blocks, tokens, width), jnp.bfloat16),
            pltpu.VMEM((blocks, 2 * per_block, 128), jnp.float32),
            pltpu.VMEM((blocks, tokens, width), jnp.bfloat16),
            pltpu.VMEM((blocks, 2 * per_block, 128), jnp.float32),
            pltpu.VMEM((blocks, tokens, width), jnp.bfloat16),
            pltpu.VMEM(w_o.shape, jnp.bfloat16),
            dma,
            dma((blocks,)),
            dma((blocks,)),
            dma((blocks,)),
            dma((blocks,)),
            dma((blocks,)),
            dma((blocks,)),
            dma((rows_gx,)),
            dma((rows_gx,)),
        ],
        compiler_params=pltpu.CompilerParams(
            collective_id=cid, has_side_effects=True, vmem_limit_bytes=48 * 1024 * 1024
        ),
        name="attention_block",
    )(
        limit, qkv, q_gain, k_gain, cosine, sine, cache_k, cache_v, tree_mask, states_here, w_o
    )


def rms_scale(values, gain):
    return values * lax.rsqrt(jnp.mean(values * values, -1, keepdims=True) + EPS) * gain


def angles_of(position, dim):
    freqs = jnp.exp(jnp.arange(dim // 2, dtype=jnp.float32) * (-2.0 * THETA_LOG / dim))
    angles = position.astype(jnp.float32)[..., None] * freqs
    cosine = jnp.cos(angles)
    sine = jnp.sin(angles)
    return jnp.concatenate([cosine, cosine], -1), jnp.concatenate([-sine, sine], -1)


def body(
    states,
    attn_gain,
    w_qkv,
    q_gain,
    k_gain,
    cache_k,
    cache_v,
    cache_len,
    tree_mask,
    w_o,
    ffn_gain,
    routing,
    route_weight,
    w_in,
    w_down,
    accept,
):
    tok_rows, model_width = states.shape
    head_dim = q_gain.shape[0]
    kv_cols = cache_k.shape[2]
    heads_all = w_o.shape[0] // head_dim
    cache_span = cache_k.shape[1]
    cols_here = w_o.shape[1]
    col_index = lax.axis_index("gy")
    row_index = lax.axis_index("gx")
    count_gx = lax.axis_size("gx")
    normed = rms_scale(states.astype(jnp.float32), attn_gain.astype(jnp.float32)).astype(
        jnp.bfloat16
    )
    qkv_part = jnp.dot(normed, w_qkv, preferred_element_type=jnp.float32).astype(jnp.bfloat16)
    (qkv_blocks,) = exchange([qkv_part], "gy", False, 0)
    qkv_whole = jnp.swapaxes(qkv_blocks, 0, 1).reshape(tok_rows, -1)
    q_cols = heads_all * head_dim
    depth = jnp.sum(tree_mask, -1) - 1
    cosine, sine = angles_of((cache_len[:, None] + depth)[0], head_dim)
    states_here = lax.dynamic_slice_in_dim(states, col_index * cols_here, cols_here, 1)
    gathered, k_rot = attention_block(
        qkv_whole,
        q_gain[None],
        k_gain[None],
        cosine,
        sine,
        cache_k[0],
        cache_v[0],
        cache_len - col_index * cache_span,
        tree_mask[0],
        states_here,
        w_o,
        1,
    )
    resid = lax.dynamic_index_in_dim(gathered, row_index, 0, False)
    exp_here = w_in.shape[0]
    expert_count = exp_here * count_gx
    top_k = routing.shape[1]
    most_rows = 3 * tok_rows * top_k // (2 * expert_count)
    hidden_units = w_down.shape[1]
    gain_float = ffn_gain.astype(jnp.float32)
    tokens = routing.shape[0]
    slots = count_gx * most_rows
    own_experts = row_index * exp_here + jnp.arange(exp_here, dtype=jnp.int32)
    matched = routing[:, None, :] == own_experts[None, :, None]
    hits = jnp.any(matched, -1)
    weights = jnp.sum(jnp.where(matched, route_weight[:, None, :], 0.0), -1)
    order = jnp.arange(tok_rows, dtype=jnp.int32)
    earlier = (order[:, None] > order[None, :]).astype(jnp.bfloat16)
    rank = jnp.einsum(
        "tu,bue->bte",
        earlier,
        hits.astype(jnp.bfloat16).reshape(count_gx, tok_rows, exp_here),
        preferred_element_type=jnp.float32,
    ).astype(jnp.int32)
    first_slot = jnp.arange(count_gx, dtype=jnp.int32)[:, None, None] * most_rows
    slot_of = jnp.where(hits, (rank + first_slot).reshape(tokens, exp_here), -1)
    pick = slot_of.T[:, None, :] == jnp.arange(slots, dtype=jnp.int32)[None, :, None]
    pick_matrix = pick.astype(jnp.bfloat16)
    slot_weight = jnp.sum(jnp.where(pick, weights.T[:, None, :], 0.0), -1)
    gathered = gathered.reshape(tokens, cols_here).astype(jnp.float32)
    token_squares = jnp.sum(gathered * gathered, -1)
    slot_squares = jnp.sum(jnp.where(pick, token_squares, 0.0), -1)
    piece = 16
    slot_squares = jnp.pad(slot_squares.reshape(-1, piece), ((0, 0), (0, 128 - piece)))
    scaled = (gathered * gain_float).astype(jnp.bfloat16)
    rows = jnp.einsum(
        "est,td->esd", pick_matrix, scaled, preferred_element_type=jnp.float32
    ).astype(jnp.bfloat16)
    layer_out = expert_layer(
        rows,
        slot_squares,
        w_in,
        w_down,
        slot_weight[..., None],
        pick_matrix.reshape(exp_here * slots, tokens).T,
        resid,
        model_width,
        4,
    )
    kv_new = jnp.concatenate([k_rot, qkv_whole[:, q_cols + kv_cols :]], -1)[None]
    accepted_kv = jnp.einsum(
        "rat,rtc->rac", accept.astype(jnp.bfloat16), kv_new, preferred_element_type=jnp.float32
    ).astype(jnp.bfloat16)
    return (layer_out, accepted_kv)


def solution(mesh):
    in_specs = (
        P("gx", None),
        P(),
        P(None, "gy"),
        P(),
        P(),
        P("gx", "gy", None),
        P("gx", "gy", None),
        P("gx"),
        P("gx", None, None),
        P(None, "gy"),
        P("gy"),
        P(),
        P(),
        P("gx", "gy", None),
        P("gx", None, "gy"),
        P("gx", None, None),
    )
    out_specs = (P("gx", "gy"), P("gx", None, None))
    return jax.shard_map(body, mesh=mesh, in_specs=in_specs, out_specs=out_specs, check_vma=False)
```

```python
import math

import jax
import jax.numpy as jnp
from jax import lax
from jax.experimental import pallas as pl
from jax.experimental.pallas import tpu as pltpu
from jax.sharding import PartitionSpec as P

EPS = 1e-06
NEG = -1e30
THETA_LOG = math.log(1000000.0)


MESH = pl.DeviceIdType.MESH


def exchange(arrays, axis, scatter, cid):
    count = lax.axis_size(axis)
    number = len(arrays)

    def kernel(*refs):
        ins, outs = refs[:number], refs[number : 2 * number]
        send, recv, local = refs[2 * number :]
        me = lax.axis_index(axis)
        barrier = pltpu.get_barrier_semaphore()
        for d in range(1, count):
            pl.semaphore_signal(
                barrier, inc=1, device_id={axis: lax.rem(me + d, count)}, device_id_type=MESH
            )
        pl.semaphore_wait(barrier, count - 1)
        copies = []
        for d in range(1, count):
            peer = lax.rem(me + d, count)
            for i in range(number):
                copy = pltpu.make_async_remote_copy(
                    src_ref=ins[i].at[peer] if scatter else ins[i],
                    dst_ref=outs[i].at[me],
                    send_sem=send.at[i, d],
                    recv_sem=recv.at[i, d],
                    device_id={axis: peer},
                    device_id_type=MESH,
                )
                copy.start()
                copies.append(copy)
        own = []
        for i in range(number):
            copy = pltpu.make_async_copy(
                ins[i].at[me] if scatter else ins[i], outs[i].at[me], local.at[i]
            )
            copy.start()
            own.append(copy)
        for copy in own + copies:
            copy.wait()

    outs = [
        jax.ShapeDtypeStruct(x.shape if scatter else (count,) + x.shape, x.dtype) for x in arrays
    ]
    return pl.pallas_call(
        kernel,
        out_shape=outs,
        in_specs=[pl.BlockSpec(memory_space=pltpu.VMEM)] * number,
        out_specs=[pl.BlockSpec(memory_space=pltpu.VMEM)] * number,
        scratch_shapes=[
            pltpu.SemaphoreType.DMA((number, count)),
            pltpu.SemaphoreType.DMA((number, count)),
            pltpu.SemaphoreType.DMA((number,)),
        ],
        compiler_params=pltpu.CompilerParams(collective_id=cid, has_side_effects=True),
        name="exchange_%d" % cid,
    )(*arrays)


def expert_layer(rows, squares, w_in, w_down, slot_weight, pick_back, resid, model_width, cid):
    axis = "gy"
    count = lax.axis_size(axis)
    peers = lax.axis_size("gx")
    experts, slots, depth = rows.shape
    tokens, cols = resid.shape
    wide = w_in.shape[2]
    units = wide // 2
    half = experts // 2
    piece = 16
    sub = slots // piece
    chunks = half * sub
    hop = 2
    far = hop * (count - 1)

    def kernel(
        x_ref, sq_ref, weight_ref, pick_ref, resid_ref, w_hbm, d_hbm, out_ref,
        hid_ref, wbuf, dbuf, part, rbuf, sqbuf, inv_ref, obuf, pbuf, ret,
        wsem, dsem, rs_s, rs_r, h_s, h_r, sq_s, sq_r, g_s, g_r,
    ):
        me = lax.axis_index(axis)
        prev = lax.rem(me + count - 1, count)
        nxt = lax.rem(me + 1, count)
        at_low = me == 0
        at_high = me == count - 1

        def load(e):
            return pltpu.make_async_copy(w_hbm.at[e], wbuf.at[e], wsem.at[e])

        def load_down(e):
            return pltpu.make_async_copy(d_hbm.at[e], dbuf.at[e], dsem.at[e])

        row = lax.axis_index("gx")
        for s in range(half):
            load(half + s).start()
            load(s).start()
        for s in range(half):
            load_down(half + s).start()
            load_down(s).start()
        barrier = pltpu.get_barrier_semaphore()
        for d in range(1, count):
            pl.semaphore_signal(
                barrier, inc=1, device_id={axis: lax.rem(me + d, count)}, device_id_type=MESH
            )
        for d in range(1, peers):
            pl.semaphore_signal(
                barrier, inc=1, device_id={"gx": lax.rem(row + d, peers)}, device_id_type=MESH
            )

        def multiply(h, s):
            e = h * half + s
            load(e).wait()
            value = jnp.dot(x_ref[e], wbuf[e], preferred_element_type=jnp.float32)
            for j in range(sub):
                part[h, s * sub + j] = value[j * piece : (j + 1) * piece].astype(jnp.bfloat16)

        multiply(1, 0)
        multiply(0, 0)
        pl.semaphore_wait(barrier, count + peers - 2)

        def sq_copy(d):
            return pltpu.make_async_remote_copy(
                src_ref=sq_ref,
                dst_ref=sqbuf.at[d],
                send_sem=sq_s.at[d],
                recv_sem=sq_r.at[d],
                device_id={axis: lax.rem(me + d, count)},
                device_id_type=MESH,
            )

        for d in range(1, count):
            sq_copy(d).start()

        def finish_squares():
            total = sq_ref[...]
            for d in range(1, count):
                sq_copy(d).wait()
                total = total + sqbuf[d]
            inv_ref[...] = lax.rsqrt(total / model_width + EPS)

        diagonal = lax.broadcasted_iota(jnp.int32, (piece, 128), 0) == lax.broadcasted_iota(
            jnp.int32, (piece, 128), 1
        )

        def rs_copy(h, c):
            return pltpu.make_async_remote_copy(
                src_ref=part.at[h, c],
                dst_ref=rbuf.at[h, c],
                send_sem=rs_s.at[h, c],
                recv_sem=rs_r.at[h, c],
                device_id={axis: nxt if h else prev},
                device_id_type=MESH,
            )

        def hid_copy(h, c):
            return pltpu.make_async_remote_copy(
                src_ref=hid_ref.at[h, c],
                dst_ref=hid_ref.at[h, c],
                send_sem=h_s.at[h, c],
                recv_sem=h_r.at[h, c],
                device_id={axis: prev if h else nxt},
                device_id_type=MESH,
            )

        def ends(h):
            return (at_low, at_high) if h else (at_high, at_low)

        def reduce_chunk(h, c):
            first, last = ends(h)

            @pl.when(jnp.logical_not(first))
            def _():
                rs_copy(h, c).wait_recv()

            @pl.when(jnp.logical_not(jnp.logical_or(first, last)))
            def _():
                part[h, c] = (
                    part[h, c].astype(jnp.float32) + rbuf[h, c].astype(jnp.float32)
                ).astype(jnp.bfloat16)

            @pl.when(jnp.logical_not(last))
            def _():
                rs_copy(h, c).start()

            @pl.when(last)
            def _():
                row = inv_ref[pl.ds(h * chunks + c, 1), :]
                inverse = jnp.sum(jnp.where(diagonal, row, 0.0), 1, keepdims=True)
                summed = part[h, c].astype(jnp.float32) + rbuf[h, c].astype(jnp.float32)
                gate = summed[:, :units] * inverse
                up = summed[:, units:] * inverse
                hid_ref[h, c] = (gate / (1.0 + jnp.exp(-gate)) * up).astype(jnp.bfloat16)
                hid_copy(h, c).start()

        def return_chunk(h, c):
            first, last = ends(h)

            @pl.when(jnp.logical_not(last))
            def _():
                hid_copy(h, c).wait_recv()

            @pl.when(jnp.logical_not(jnp.logical_or(first, last)))
            def _():
                hid_copy(h, c).start()

        def project(h, s):
            e = h * half + s
            load_down(e).wait()
            value = hid_ref[h, pl.ds(s * sub, sub)].reshape(slots, units)
            value = jnp.dot(value, dbuf[e], preferred_element_type=jnp.float32)
            obuf[e] = (value * weight_ref[e]).astype(jnp.bfloat16)

        def step(t, carry):
            for h, place in ((1, 1), (0, sub // 2 + 1)):

                @pl.when(jnp.logical_and(t < chunks - sub, lax.rem(t, sub) == place))
                def _():
                    multiply(h, lax.div(t, sub) + 1)

            @pl.when(t == far - 1)
            def _():
                finish_squares()

            for h in (1, 0):
                way = hop * (me if h else count - 1 - me)
                c = t - way

                @pl.when(jnp.logical_and(c >= 0, c < chunks))
                def _():
                    reduce_chunk(h, c)

            for h in (1, 0):
                way = hop * (me if h else count - 1 - me)
                b = t - 2 * far + way

                @pl.when(jnp.logical_and(b >= 0, b < chunks))
                def _():
                    return_chunk(h, b)

                    @pl.when(lax.rem(b, sub) == sub - 1)
                    def _():
                        project(h, lax.div(b, sub))

            return carry

        lax.fori_loop(0, chunks + 2 * far, step, 0)

        def finish(c, carry):
            for h in (1, 0):
                first, last = ends(h)

                @pl.when(jnp.logical_not(last))
                def _():
                    rs_copy(h, c).wait_send()

                @pl.when(jnp.logical_not(first))
                def _():
                    hid_copy(h, c).wait_send()

            return carry

        summed = lax.dot_general(
            pick_ref[...],
            obuf[...].reshape(experts * slots, cols),
            (((0,), (0,)), ((), ())),
            preferred_element_type=jnp.float32,
        )
        for p in range(peers):
            pbuf[p] = summed[p * tokens : (p + 1) * tokens].astype(jnp.bfloat16)

        def back_copy(d):
            peer = lax.rem(row + d, peers)
            return pltpu.make_async_remote_copy(
                src_ref=pbuf.at[peer],
                dst_ref=ret.at[d],
                send_sem=g_s.at[d],
                recv_sem=g_r.at[d],
                device_id={"gx": peer},
                device_id_type=MESH,
            )

        for d in range(1, peers):
            back_copy(d).start()
        moe = pbuf[row].astype(jnp.float32)
        lax.fori_loop(0, chunks, finish, 0)
        for d in range(1, peers):
            back_copy(d).wait_recv()
            moe = moe + ret[d].astype(jnp.float32)
        out_ref[...] = (resid_ref[...].astype(jnp.float32) + moe).astype(jnp.bfloat16)
        for d in range(1, peers):
            back_copy(d).wait_send()

    vmem = pl.BlockSpec(memory_space=pltpu.VMEM)
    hbm = pl.BlockSpec(memory_space=pl.ANY)
    dma = pltpu.SemaphoreType.DMA
    return pl.pallas_call(
        kernel,
        out_shape=jax.ShapeDtypeStruct((tokens, cols), jnp.bfloat16),
        in_specs=[vmem] * 5 + [hbm, hbm],
        out_specs=vmem,
        scratch_shapes=[
            pltpu.VMEM((2, chunks, piece, units), jnp.bfloat16),
            pltpu.VMEM((experts, depth, wide), jnp.bfloat16),
            pltpu.VMEM((experts, units, cols), jnp.bfloat16),
            pltpu.VMEM((2, chunks, piece, wide), jnp.bfloat16),
            pltpu.VMEM((2, chunks, piece, wide), jnp.bfloat16),
            pltpu.VMEM((count, 2 * chunks, 128), jnp.float32),
            pltpu.VMEM((2 * chunks, 128), jnp.float32),
            pltpu.VMEM((experts, slots, cols), jnp.bfloat16),
            pltpu.VMEM((peers, tokens, cols), jnp.bfloat16),
            pltpu.VMEM((peers, tokens, cols), jnp.bfloat16),
            dma((experts,)),
            dma((experts,)),
            dma((2, chunks)),
            dma((2, chunks)),
            dma((2, chunks)),
            dma((2, chunks)),
            dma((count,)),
            dma((count,)),
            dma((peers,)),
            dma((peers,)),
        ],
        compiler_params=pltpu.CompilerParams(
            collective_id=cid, has_side_effects=True, vmem_limit_bytes=52 * 1024 * 1024
        ),
        name="expert_layer",
    )(rows, squares, slot_weight, pick_back, resid, w_in, w_down)


def attention_block(
    qkv, q_gain, k_gain, cosine, sine, cache_k, cache_v, limit, tree_mask, states_here, w_o, cid
):
    blocks = lax.axis_size("gy")
    rows_gx = lax.axis_size("gx")
    tokens = qkv.shape[0]
    span, kv_cols = cache_k.shape
    dim = q_gain.shape[1]
    kv_heads = kv_cols // dim
    heads = qkv.shape[1] // dim - 2 * kv_heads
    group = heads // kv_heads
    per_block = heads // blocks
    blocks_here = blocks // kv_heads
    width = per_block * dim
    cols = w_o.shape[1]
    scale = dim ** (-0.5)

    def kernel(
        limit_ref, q_ref, qg_ref, kg_ref, cos_ref, sin_ref, k_ref, v_ref, mask_ref, st_ref, wo_hbm,
        h_ref, rot_ref,
        acc_out, stat_out, acc_in, stat_in, attn, wo,
        wo_sem, a_s, a_r, s_s, s_r, t_s, t_r, h_s, h_r,
    ):
        me = lax.axis_index("gy")
        row = lax.axis_index("gx")
        load = pltpu.make_async_copy(wo_hbm, wo, wo_sem)
        load.start()
        barrier = pltpu.get_barrier_semaphore()
        for axis, here, count in (("gy", me, blocks), ("gx", row, rows_gx)):
            for d in range(1, count):
                pl.semaphore_signal(
                    barrier, inc=1, device_id={axis: lax.rem(here + d, count)}, device_id_type=MESH
                )
        pl.semaphore_wait(barrier, blocks + rows_gx - 2)

        def send(src, dst, send_sem, recv_sem, axis, peer):
            return pltpu.make_async_remote_copy(
                src_ref=src,
                dst_ref=dst,
                send_sem=send_sem,
                recv_sem=recv_sem,
                device_id={axis: peer},
                device_id_type=MESH,
            )

        def part_copies(block, source):
            return (
                send(acc_out.at[block], acc_in.at[source], a_s.at[block], a_r.at[source], "gy", block),
                send(stat_out.at[block], stat_in.at[source], s_s.at[block], s_r.at[source], "gy", block),
            )

        cos = cos_ref[...]
        sin = sin_ref[...]

        def turn(value, gain):
            value = value.astype(jnp.float32)
            value = value * lax.rsqrt(jnp.mean(value * value, -1, keepdims=True) + EPS) * gain
            return (value * cos + pltpu.roll(value, dim // 2, 1) * sin).astype(jnp.bfloat16)

        q_gain_row = qg_ref[...].astype(jnp.float32)
        k_gain_row = kg_ref[...].astype(jnp.float32)
        contract = (((1,), (1,)), ((), ()))
        diagonal = lax.broadcasted_iota(jnp.int32, (tokens, 128), 0) == lax.broadcasted_iota(
            jnp.int32, (tokens, 128), 1
        )

        def one_head(i, carry):
            g = lax.rem(lax.div(me, blocks_here) + 1 + i, kv_heads)

            def lanes(first, size):
                return pl.ds(pl.multiple_of(first, 128), size)

            query = jnp.concatenate(
                [
                    turn(q_ref[:, lanes((g * group + j) * dim, dim)], q_gain_row)
                    for j in range(group)
                ],
                0,
            )
            keys = turn(q_ref[:, lanes((heads + g) * dim, dim)], k_gain_row)
            values = q_ref[:, lanes((heads + kv_heads + g) * dim, dim)]
            rot_ref[:, lanes(g * dim, dim)] = keys
            tree = (
                lax.dot_general(query, keys, contract, preferred_element_type=jnp.float32) * scale
            )
            mask = jnp.concatenate([mask_ref[...]] * group, 0)
            tree_ok = jnp.logical_and(mask == 1, me == 0)
            tree = jnp.where(tree_ok, tree, NEG)
            score = (
                lax.dot_general(
                    query,
                    k_ref[:, lanes(g * dim, dim)],
                    contract,
                    preferred_element_type=jnp.float32,
                )
                * scale
            )
            valid = lax.broadcasted_iota(jnp.int32, score.shape, 1) < limit_ref[0]
            score = jnp.where(valid, score, NEG)
            top = jnp.maximum(jnp.max(score, 1, keepdims=True), jnp.max(tree, 1, keepdims=True))
            prob = jnp.where(valid, jnp.exp(score - top), 0.0).astype(jnp.bfloat16)
            prob_tree = jnp.where(tree_ok, jnp.exp(tree - top), 0.0).astype(jnp.bfloat16)
            total = jnp.sum(prob.astype(jnp.float32), 1, keepdims=True) + jnp.sum(
                prob_tree.astype(jnp.float32), 1, keepdims=True
            )
            acc = jnp.dot(prob, v_ref[:, lanes(g * dim, dim)], preferred_element_type=jnp.float32)
            acc = acc + jnp.dot(prob_tree, values, preferred_element_type=jnp.float32)
            acc = acc.astype(jnp.bfloat16)
            for b in range(blocks_here):
                block = g * blocks_here + b
                for place in range(per_block):
                    j = b * per_block + place
                    rows = slice(j * tokens, (j + 1) * tokens)
                    acc_out[block, :, place * dim : (place + 1) * dim] = acc[rows]
                    for k, column in enumerate((top, total)):
                        stat_out[block, k * per_block + place : k * per_block + place + 1, :] = (
                            jnp.sum(jnp.where(diagonal, column[rows], 0.0), 0, keepdims=True)
                        )

                @pl.when(block != me)
                def _():
                    for copy in part_copies(block, me):
                        copy.start()

            return carry

        lax.fori_loop(0, kv_heads, one_head, 0)

        acc_in[me] = acc_out[me]
        stat_in[me] = stat_out[me]
        for d in range(1, blocks):
            source = lax.rem(me + d, blocks)
            for copy in part_copies(source, source):
                copy.wait_recv()
        tops = [stat_in[j, :per_block, :] for j in range(blocks)]
        best = tops[0]
        for j in range(1, blocks):
            best = jnp.maximum(best, tops[j])
        factors = [jnp.exp(tops[j] - best) for j in range(blocks)]
        denom = stat_in[0, per_block:, :] * factors[0]
        for j in range(1, blocks):
            denom = denom + stat_in[j, per_block:, :] * factors[j]
        for place in range(per_block):
            joined = jnp.zeros((tokens, dim), jnp.float32)
            for j in range(blocks):
                line = (factors[j] / denom)[place : place + 1, :]
                column = jnp.sum(jnp.where(diagonal, line, 0.0), 1, keepdims=True)
                joined = joined + column * acc_in[
                    j, :, place * dim : (place + 1) * dim
                ].astype(jnp.float32)
            attn[me, :, place * dim : (place + 1) * dim] = joined.astype(jnp.bfloat16)

        def attn_copy(d, source):
            return send(
                attn.at[source], attn.at[source], t_s.at[d], t_r.at[d], "gy", lax.rem(me + d, blocks)
            )

        for d in range(1, blocks):
            attn_copy(d, me).start()
        load.wait()

        def project(source):
            return jnp.dot(
                attn[source],
                wo[pl.ds(pl.multiple_of(source * width, width), width), :],
                preferred_element_type=jnp.float32,
            )

        total = st_ref[...].astype(jnp.float32) + project(me)
        for d in range(1, blocks):
            source = lax.rem(me + blocks - d, blocks)
            attn_copy(d, source).wait_recv()
            total = total + project(source)
        h_ref[row] = total.astype(jnp.bfloat16)

        def h_copy(d, source):
            return send(
                h_ref.at[source], h_ref.at[source], h_s.at[d], h_r.at[d], "gx",
                lax.rem(row + d, rows_gx),
            )

        for d in range(1, rows_gx):
            h_copy(d, row).start()
        for d in range(1, blocks):
            block = lax.rem(me + d, blocks)
            for copy in part_copies(block, me):
                copy.wait_send()
            attn_copy(d, me).wait_send()
        for d in range(1, rows_gx):
            h_copy(d, lax.rem(row + rows_gx - d, rows_gx)).wait_recv()
            h_copy(d, row).wait_send()

    vmem = pl.BlockSpec(memory_space=pltpu.VMEM)
    dma = pltpu.SemaphoreType.DMA
    return pl.pallas_call(
        kernel,
        out_shape=[
            jax.ShapeDtypeStruct((rows_gx, tokens, cols), jnp.bfloat16),
            jax.ShapeDtypeStruct((tokens, kv_cols), jnp.bfloat16),
        ],
        in_specs=[pl.BlockSpec(memory_space=pltpu.SMEM)]
        + [vmem] * 9
        + [pl.BlockSpec(memory_space=pl.ANY)],
        out_specs=[vmem, vmem],
        scratch_shapes=[
            pltpu.VMEM((blocks, tokens, width), jnp.bfloat16),
            pltpu.VMEM((blocks, 2 * per_block, 128), jnp.float32),
            pltpu.VMEM((blocks, tokens, width), jnp.bfloat16),
            pltpu.VMEM((blocks, 2 * per_block, 128), jnp.float32),
            pltpu.VMEM((blocks, tokens, width), jnp.bfloat16),
            pltpu.VMEM(w_o.shape, jnp.bfloat16),
            dma,
            dma((blocks,)),
            dma((blocks,)),
            dma((blocks,)),
            dma((blocks,)),
            dma((blocks,)),
            dma((blocks,)),
            dma((rows_gx,)),
            dma((rows_gx,)),
        ],
        compiler_params=pltpu.CompilerParams(
            collective_id=cid, has_side_effects=True, vmem_limit_bytes=48 * 1024 * 1024
        ),
        name="attention_block",
    )(
        limit, qkv, q_gain, k_gain, cosine, sine, cache_k, cache_v, tree_mask, states_here, w_o
    )


def rms_scale(values, gain):
    return values * lax.rsqrt(jnp.mean(values * values, -1, keepdims=True) + EPS) * gain


def angles_of(position, dim):
    freqs = jnp.exp(jnp.arange(dim // 2, dtype=jnp.float32) * (-2.0 * THETA_LOG / dim))
    angles = position.astype(jnp.float32)[..., None] * freqs
    cosine = jnp.cos(angles)
    sine = jnp.sin(angles)
    return jnp.concatenate([cosine, cosine], -1), jnp.concatenate([-sine, sine], -1)


def body(
    states,
    attn_gain,
    w_qkv,
    q_gain,
    k_gain,
    cache_k,
    cache_v,
    cache_len,
    tree_mask,
    w_o,
    ffn_gain,
    routing,
    route_weight,
    w_in,
    w_down,
    accept,
):
    tok_rows, model_width = states.shape
    head_dim = q_gain.shape[0]
    kv_cols = cache_k.shape[2]
    heads_all = w_o.shape[0] // head_dim
    cache_span = cache_k.shape[1]
    cols_here = w_o.shape[1]
    col_index = lax.axis_index("gy")
    row_index = lax.axis_index("gx")
    count_gx = lax.axis_size("gx")
    normed = rms_scale(states.astype(jnp.float32), attn_gain.astype(jnp.float32)).astype(
        jnp.bfloat16
    )
    qkv_part = jnp.dot(normed, w_qkv, preferred_element_type=jnp.float32).astype(jnp.bfloat16)
    (qkv_blocks,) = exchange([qkv_part], "gy", False, 0)
    qkv_whole = jnp.swapaxes(qkv_blocks, 0, 1).reshape(tok_rows, -1)
    q_cols = heads_all * head_dim
    depth = jnp.sum(tree_mask, -1) - 1
    cosine, sine = angles_of((cache_len[:, None] + depth)[0], head_dim)
    states_here = lax.dynamic_slice_in_dim(states, col_index * cols_here, cols_here, 1)
    gathered, k_rot = attention_block(
        qkv_whole,
        q_gain[None],
        k_gain[None],
        cosine,
        sine,
        cache_k[0],
        cache_v[0],
        cache_len - col_index * cache_span,
        tree_mask[0],
        states_here,
        w_o,
        1,
    )
    resid = lax.dynamic_index_in_dim(gathered, row_index, 0, False)
    exp_here = w_in.shape[0]
    expert_count = exp_here * count_gx
    top_k = routing.shape[1]
    most_rows = 3 * tok_rows * top_k // (2 * expert_count)
    hidden_units = w_down.shape[1]
    gain_float = ffn_gain.astype(jnp.float32)
    tokens = routing.shape[0]
    slots = count_gx * most_rows
    own_experts = row_index * exp_here + jnp.arange(exp_here, dtype=jnp.int32)
    matched = routing[:, None, :] == own_experts[None, :, None]
    hits = jnp.any(matched, -1)
    weights = jnp.sum(jnp.where(matched, route_weight[:, None, :], 0.0), -1)
    order = jnp.arange(tok_rows, dtype=jnp.int32)
    earlier = (order[:, None] > order[None, :]).astype(jnp.bfloat16)
    rank = jnp.einsum(
        "tu,bue->bte",
        earlier,
        hits.astype(jnp.bfloat16).reshape(count_gx, tok_rows, exp_here),
        preferred_element_type=jnp.float32,
    ).astype(jnp.int32)
    first_slot = jnp.arange(count_gx, dtype=jnp.int32)[:, None, None] * most_rows
    slot_of = jnp.where(hits, (rank + first_slot).reshape(tokens, exp_here), -1)
    pick = slot_of.T[:, None, :] == jnp.arange(slots, dtype=jnp.int32)[None, :, None]
    pick_matrix = pick.astype(jnp.bfloat16)
    slot_weight = jnp.sum(jnp.where(pick, weights.T[:, None, :], 0.0), -1)
    gathered = gathered.reshape(tokens, cols_here).astype(jnp.float32)
    token_squares = jnp.sum(gathered * gathered, -1)
    slot_squares = jnp.sum(jnp.where(pick, token_squares, 0.0), -1)
    piece = 16
    slot_squares = jnp.pad(slot_squares.reshape(-1, piece), ((0, 0), (0, 128 - piece)))
    scaled = (gathered * gain_float).astype(jnp.bfloat16)
    rows = jnp.einsum(
        "est,td->esd", pick_matrix, scaled, preferred_element_type=jnp.float32
    ).astype(jnp.bfloat16)
    layer_out = expert_layer(
        rows,
        slot_squares,
        w_in,
        w_down,
        slot_weight[..., None],
        pick_matrix.reshape(exp_here * slots, tokens),
        resid,
        model_width,
        4,
    )
    kv_new = jnp.concatenate([k_rot, qkv_whole[:, q_cols + kv_cols :]], -1)[None]
    accepted_kv = jnp.einsum(
        "rat,rtc->rac", accept.astype(jnp.bfloat16), kv_new, preferred_element_type=jnp.float32
    ).astype(jnp.bfloat16)
    return (layer_out, accepted_kv)


def solution(mesh):
    in_specs = (
        P("gx", None),
        P(),
        P(None, "gy"),
        P(),
        P(),
        P("gx", "gy", None),
        P("gx", "gy", None),
        P("gx"),
        P("gx", None, None),
        P(None, "gy"),
        P("gy"),
        P(),
        P(),
        P("gx", "gy", None),
        P("gx", None, "gy"),
        P("gx", None, None),
    )
    out_specs = (P("gx", "gy"), P("gx", None, None))
    return jax.shard_map(body, mesh=mesh, in_specs=in_specs, out_specs=out_specs, check_vma=False)
```
